128 devices in a mesh: list: 32 (over x, z, core), help: 4 (over y).
Axes of the slice: x: 4, y: 4, z: 4, core: 2. Of those that a mesh axis runs over, the one named last changes fastest.
Arguments:
- members: bfloat16 [524288, 768], P(('list', 'help')), may hold values from -6 to 6
- owner: int32 [524288, 1], P(('list', 'help')), may hold values from 0 to 63; in each aligned block of 4096 rows (0 to 4095, 4096 to 8191, ...) at most 128 rows name the same one
- seed_label: int32 [524288], P(('list', 'help')), may hold values from 0 to 7
Outputs:
- assignments: float32 [8, 524288], P(None, ('list', 'help'))
- centroids: float32 [64, 8, 768], P('list')
The draws below stay inside these ranges and needn't reach their ends.
Inputs may be any that keep to these rules, and one draw needn't show every extreme that they name: `owner`: in each device's block of 4096 members no list is named by more than 128 of them, a bound that some block reaches; every list has members.
All inputs are finite; a program needn't handle non-finite values.
Results may differ from the reference program's by a relative error of at most 0.012.
The reference program's roundings to bfloat16 on the way count: a program that leaves them out, or rounds other values in their place, can miss the bound.
Values may be sent and summed in bfloat16 or wider, within the bound.
No kernel may reach another device: no remote copies, remote signals or barrier semaphores. Data moves between devices by JAX's collectives and lax.ppermute only.
A program may use at most 128 MiB of HBM per device.

```python
import math
import jax
import jax.numpy as jnp
import numpy as np
from jax import lax

D = 768
K = 8
ITERS = 3
MEM_DEV = 4096
LISTS = 64
CAP = 128
MEMBERS = 524288


def draw_members(key, part):
    keys = jax.random.split(key, 1)
    values = jnp.clip(jax.random.normal(keys[0], (MEMBERS, D), jnp.float32), -6.0, 6.0)
    return values.astype(jnp.bfloat16)


def place_ends(drawn, rng, least, top_value):
    extent = drawn.shape
    spot = [jax.random.randint(jax.random.fold_in(rng, axis), (), 0, extent[axis]) for axis in range(len(extent))]
    drawn = drawn.at[tuple(spot)].set(least)
    longest = extent.index(max(extent))
    spot[longest] = (spot[longest] + 1) % extent[longest]
    return drawn.at[tuple(spot)].set(top_value)


def deal_out(rng, own, number, rows, count, top, limit, lean):
    sequence = jax.random.permutation(rng, count)
    packed, common = portions_of(count, rows * top, limit, lean, True), portions_of(count, rows * top, limit, lean, False)
    places = jnp.arange(count)

    def named(tallies, offset_by):
        used = int((tallies > 0).sum())
        fixed = max(1, used // 4)
        passed = fixed + (places - fixed + offset_by * (used - fixed)) % max(1, count - fixed)
        return jnp.zeros((count,), jnp.int32).at[sequence[jnp.where(places < fixed, places, passed)]].set(jnp.asarray(tallies, jnp.int32))

    tallies = jnp.where(number % 4 == 0, named(packed, number // 4), named(common, number - number // 4 - 1))
    mixed = jax.random.permutation(jax.random.fold_in(own, 3), count)
    giver, receiver = mixed[0:count // 2 * 2:2], mixed[1:count // 2 * 2:2]
    room = jnp.minimum(tallies[giver] - 1, limit - tallies[receiver]) // 2
    room = jnp.where((giver == sequence[0]) | (receiver == sequence[0]) | (tallies[receiver] == 0), 0, jnp.maximum(room, 0))
    passed = jax.random.randint(jax.random.fold_in(own, 4), (count // 2,), 0, 1 << 20) % (room + 1)
    tallies = tallies.at[giver].add(-passed).at[receiver].add(passed)
    labels = jnp.searchsorted(jnp.cumsum(tallies), jnp.arange(rows * top), side="right").astype(jnp.int32)
    listing = labels.reshape(top, rows).T
    listing = listing[jax.random.permutation(jax.random.fold_in(own, 1), rows)]
    offset_by = jax.random.randint(jax.random.fold_in(own, 2), (rows, 1), 0, top)
    return jnp.take_along_axis(listing, (jnp.arange(top)[None, :] + offset_by) % top, axis=1)


def portions_of(amount, total, limit, slope, full):
    portions = [(1 << 20) // math.isqrt(rank ** slope) + 1 for rank in range(1, amount + 1)]
    largest = limit if full else min(limit, max(-(-total // amount), total * portions[0] // sum(portions)))
    least = 1 if total - largest >= amount - 1 else 0
    holding, spare = [largest] + [least] * (amount - 1), total - largest - least * (amount - 1)
    while spare > 0:
        movable = [i for i in range(1, amount) if holding[i] < largest] or [i for i in range(1, amount) if holding[i] < limit]
        whole, remaining = sum([portions[i] for i in movable]), spare
        for i in movable:
            more = min(limit - holding[i], max(1, remaining * portions[i] // whole), spare)
            holding[i] = holding[i] + more
            spare = spare - more
    return np.array(holding)


def setup_inputs(seed: int = 0) -> dict:
    key_list = jax.random.split(jax.random.key(seed), 4)
    members = draw_members(jax.random.fold_in(key_list[3], 71), 0)
    owner_keys = jax.random.split(jax.random.fold_in(key_list[1], 1), MEMBERS // MEM_DEV)
    owner_turns = jax.random.permutation(jax.random.fold_in(key_list[1], 3), MEMBERS // MEM_DEV)
    owner = jax.vmap(lambda own, number: deal_out(jax.random.fold_in(key_list[1], 2), own, number, MEM_DEV, LISTS, 1, CAP, 2))(owner_keys, owner_turns).reshape((MEMBERS, 1))
    seed_label = place_ends(jax.random.randint(key_list[2], (MEMBERS,), 0, K), jax.random.fold_in(key_list[2], 1), 0, K - 1).astype(jnp.int32)
    return dict(members=members, owner=owner, seed_label=seed_label)


smoothing_heat_factor = 2.0


def soft_assign(block_vectors, tile_holder_entries, centers):
    center_bf = centers.astype(jnp.bfloat16)
    center_bf = lax.optimization_barrier(center_bf).astype(jnp.float32)
    centroid_magnitude_power = jnp.sum(centers * centers, axis=-1)
    chosen_subcentroid = center_bf[tile_holder_entries]
    separation_measures = jnp.einsum("yu,yru->yr", block_vectors.astype(jnp.float32), chosen_subcentroid, precision=lax.Precision.HIGHEST)
    membership_raw_preference = (2.0 * separation_measures - centroid_magnitude_power[tile_holder_entries]) / smoothing_heat_factor
    return jax.nn.softmax(membership_raw_preference, axis=-1)


def reference(members, owner, seed_label):
    own_ids = owner[:, 0]
    blocks = MEMBERS // MEM_DEV
    block_vectors = members.reshape(blocks, MEM_DEV, D)
    tile_holder_entries = own_ids.reshape(blocks, MEM_DEV)
    block_lab = seed_label.reshape(blocks, MEM_DEV)
    groups = jnp.arange(K, dtype=jnp.int32)

    def accumulate(centers, first):
        def step(carry, item):
            sums, totals = carry
            part_x, part_own, part_lab = item
            if first:
                weights = (part_lab[:, None] == groups[None, :]).astype(jnp.float32)
            else:
                weights = soft_assign(part_x, part_own, centers).astype(jnp.bfloat16)
                weights = lax.optimization_barrier(weights).astype(jnp.float32)
            seg_ids = (part_own[:, None] * K + groups[None, :]).reshape(-1).astype(jnp.int32)
            data = (weights[:, :, None] * part_x.astype(jnp.float32)[:, None, :]).reshape(-1, D)
            sums = sums + jax.ops.segment_sum(data, seg_ids, num_segments=LISTS * K)
            totals = totals + jax.ops.segment_sum(weights.reshape(-1), seg_ids, num_segments=LISTS * K)
            return (sums, totals), None

        start = (jnp.zeros((LISTS * K, D), jnp.float32), jnp.zeros((LISTS * K,), jnp.float32))
        (sums, totals), _ = lax.scan(step, start, (block_vectors, tile_holder_entries, block_lab))
        return (sums / (totals + 1.0)[:, None]).reshape(LISTS, K, D)

    centers = accumulate(jnp.zeros((LISTS, K, D), jnp.float32), True)
    for turn in range(ITERS):
        centers = accumulate(centers, False)
    final = lax.map(lambda item: soft_assign(item[0], item[1], centers), (block_vectors, tile_holder_entries))
    assignments = final.reshape(MEMBERS, K).T
    return assignments, centers
```

```python
import jax
import jax.numpy as jnp
from jax import lax
from jax.experimental import pallas as pl
from jax.experimental.pallas import tpu as pltpu
from jax.sharding import Mesh, PartitionSpec as P

K = 8
D = 768
ITERS = 3
HALF_D = D // 2
LANES = 128
CHUNK = HALF_D + LANES
OWN_LISTS = 32
SEATS = 64
TILE = 512
f32 = jnp.float32
bf16 = jnp.bfloat16


def lane_fold(block):
    total = block[:, :LANES]
    for at in range(LANES, block.shape[1], LANES):
        total = total + block[:, at : at + LANES]
    return total


def store_sums(out, acc, tot, base):
    for seat in range(SEATS):
        row, half = base + (seat // 2) * K, seat % 2
        out[seat, :, :HALF_D] = acc[row : row + K, half * HALF_D : (half + 1) * HALF_D]
        out[seat, :, HALF_D:] = tot[row : row + K, :]


def seed_kernel(members, code, mine, theirs, acc, tot):
    step = pl.program_id(0)

    @pl.when(step == 0)
    def _():
        acc[...] = jnp.zeros_like(acc)
        tot[...] = jnp.zeros_like(tot)

    groups = lax.broadcasted_iota(jnp.int32, (K, TILE), 0)
    shifted = jnp.broadcast_to(code[...], (K, TILE)) - groups
    rows = []
    for name in range(2 * OWN_LISTS):
        hot = jnp.where(shifted == name * K, 1.0, 0.0).astype(f32)
        tot[name * K : (name + 1) * K, :] += lane_fold(hot)
        rows.append(hot)
    hots = jnp.concatenate(rows, axis=0).astype(bf16)
    acc[...] += jnp.dot(hots, members[...], preferred_element_type=f32)

    @pl.when(step == pl.num_programs(0) - 1)
    def _():
        store_sums(mine, acc, tot, 0)
        store_sums(theirs, acc, tot, OWN_LISTS * K)


def seed_sums(members, code):
    rows = members.shape[0]
    part = jax.ShapeDtypeStruct((SEATS, K, CHUNK), f32)
    whole = pl.BlockSpec((SEATS, K, CHUNK), lambda i: (0, 0, 0))
    return pl.pallas_call(
        seed_kernel,
        grid=(rows // TILE,),
        in_specs=[
            pl.BlockSpec((TILE, D), lambda i: (i, 0)),
            pl.BlockSpec((1, TILE), lambda i: (0, i)),
        ],
        out_specs=[whole, whole],
        out_shape=[part, part],
        scratch_shapes=[
            pltpu.VMEM((2 * OWN_LISTS * K, D), f32),
            pltpu.VMEM((2 * OWN_LISTS * K, LANES), f32),
        ],
        name="seed_sums",
    )(members, code)


def finish_kernel(parts, out):
    total = parts[0]
    for seat in range(1, SEATS):
        total = total + parts[seat]
    count = jnp.sum(total[:, HALF_D:], axis=1, keepdims=True)
    centers = total[:, :HALF_D] / (count + 1.0)
    norm = jnp.sum(centers * centers, axis=1, keepdims=True)
    lane = lax.broadcasted_iota(jnp.int32, (K, LANES), 1)
    norms = jnp.broadcast_to(norm, (K, LANES))
    if out.dtype == bf16:
        high = norms.astype(bf16).astype(f32)
        middle = (norms - high).astype(bf16).astype(f32)
        low = norms - high - middle
        tail = jnp.where(lane == 0, high, jnp.where(lane == 1, middle, jnp.where(lane == 2, low, 0.0)))
    else:
        tail = jnp.where(lane == 0, norms, 0.0)
    block = jnp.concatenate([centers, tail], axis=1).astype(out.dtype)
    for seat in range(SEATS):
        out[seat] = block


def finish(parts, dtype):
    return pl.pallas_call(
        finish_kernel,
        out_shape=jax.ShapeDtypeStruct((SEATS, K, CHUNK), dtype),
        name="finish_" + jnp.dtype(dtype).name,
    )(parts)


def unpack_centers(packed, cen, nrm):
    for pair in range(OWN_LISTS // 2):
        for half in range(2):
            blocks = [packed[4 * pair + 2 * i + half].astype(f32) for i in range(2)]
            cen[pair * 16 : pair * 16 + 16, half * HALF_D : (half + 1) * HALF_D] = jnp.concatenate(
                [b[:, :HALF_D] for b in blocks], axis=0
            ).astype(bf16)
        for i in range(2):
            name = 2 * pair + i
            tails = packed[2 * name][:, HALF_D:].astype(f32) + packed[2 * name + 1][:, HALF_D:].astype(f32)
            nrm[name * K : (name + 1) * K, :] = jnp.broadcast_to(
                jnp.sum(tails, axis=1, keepdims=True), (K, LANES)
            )


def soft_weights(members, owner, cen, nrm):
    dots = lax.dot_general(
        cen[...], members[...], (((1,), (1,)), ((), ())), preferred_element_type=f32
    )
    names = jnp.broadcast_to(owner[...], (K, TILE))
    dot = jnp.zeros((K, TILE), f32)
    norm = jnp.zeros((K, TILE), f32)
    for name in range(OWN_LISTS):
        here = names == name
        rows = slice(name * K, (name + 1) * K)
        dot = jnp.where(here, dots[rows, :], dot)
        norm = jnp.where(here, jnp.concatenate([nrm[rows, :]] * (TILE // LANES), axis=1), norm)
    logits = (2.0 * dot - norm) / 2.0
    exps = jnp.exp(logits - jnp.max(logits, axis=0, keepdims=True))
    return exps / jnp.sum(exps, axis=0, keepdims=True), names


def round_kernel(packed, own, own_owner, other, other_owner, out, cen, nrm, acc, tot):
    step = pl.program_id(0)
    steps = pl.num_programs(0)

    @pl.when(step == 0)
    def _():
        unpack_centers(packed, cen, nrm)
        acc[...] = jnp.zeros_like(acc)
        tot[...] = jnp.zeros_like(tot)

    def work(members, owner):
        weights, names = soft_weights(members, owner, cen, nrm)
        weights = weights.astype(bf16).astype(f32)
        rows = []
        for name in range(OWN_LISTS):
            here = jnp.where(names == name, weights, 0.0)
            tot[name * K : (name + 1) * K, :] += lane_fold(here)
            rows.append(here)
        spread = jnp.concatenate(rows, axis=0).astype(bf16)
        acc[...] += jnp.dot(spread, members[...], preferred_element_type=f32)

    @pl.when(step < steps // 2)
    def _():
        work(own, own_owner)

    @pl.when(step >= steps // 2)
    def _():
        work(other, other_owner)

    @pl.when(step == steps - 1)
    def _():
        store_sums(out, acc, tot, 0)


def round_sums(packed, own, own_owner, other, other_owner):
    half = own.shape[0] // TILE
    first = lambda i: jnp.minimum(i, half - 1)
    second = lambda i: jnp.maximum(i - half, 0)
    whole = pl.BlockSpec((SEATS, K, CHUNK), lambda i: (0, 0, 0))
    return pl.pallas_call(
        round_kernel,
        grid=(2 * half,),
        in_specs=[
            whole,
            pl.BlockSpec((TILE, D), lambda i: (first(i), 0)),
            pl.BlockSpec((1, TILE), lambda i: (0, first(i))),
            pl.BlockSpec((TILE, D), lambda i: (second(i), 0)),
            pl.BlockSpec((1, TILE), lambda i: (0, second(i))),
        ],
        out_specs=whole,
        out_shape=jax.ShapeDtypeStruct((SEATS, K, CHUNK), f32),
        scratch_shapes=[
            pltpu.VMEM((OWN_LISTS * K, D), bf16),
            pltpu.VMEM((OWN_LISTS * K, LANES), f32),
            pltpu.VMEM((OWN_LISTS * K, D), f32),
            pltpu.VMEM((OWN_LISTS * K, LANES), f32),
        ],
        name="round_sums",
    )(packed, own, own_owner, other, other_owner)


def assign_kernel(packed, members, owner, out, cen, nrm):
    @pl.when(pl.program_id(0) == 0)
    def _():
        unpack_centers(packed, cen, nrm)

    out[...] = soft_weights(members, owner, cen, nrm)[0]


def assign(packed, members, owner):
    rows = members.shape[0]
    return pl.pallas_call(
        assign_kernel,
        grid=(rows // TILE,),
        in_specs=[
            pl.BlockSpec((SEATS, K, CHUNK), lambda i: (0, 0, 0)),
            pl.BlockSpec((TILE, D), lambda i: (i, 0)),
            pl.BlockSpec((1, TILE), lambda i: (0, i)),
        ],
        out_specs=pl.BlockSpec((K, TILE), lambda i: (0, i)),
        out_shape=jax.ShapeDtypeStruct((K, rows), f32),
        scratch_shapes=[
            pltpu.VMEM((OWN_LISTS * K, D), bf16),
            pltpu.VMEM((OWN_LISTS * K, LANES), f32),
        ],
        name="assign",
    )(packed, members, owner)


SWAP = [(0, 1), (1, 0)]
SEAT_AXES = ("x", "z", "y")


def local(members, owner, seed_label):
    core = lax.axis_index("c")
    owner = owner.reshape(1, -1)

    def relative(names):
        away = ((names >> 1) & 1) ^ core
        return (names >> 2) * 2 + (names & 1) + OWN_LISTS * away

    other = lax.ppermute(members, "c", SWAP)
    other_owner = relative(lax.ppermute(owner, "c", SWAP))
    own_owner = relative(owner)

    def exchange(parts):
        return lax.all_to_all(parts, SEAT_AXES, split_axis=0, concat_axis=0, tiled=True)

    mine, theirs = seed_sums(members, own_owner * K + seed_label.reshape(1, -1))
    parts = mine + lax.ppermute(theirs, "c", SWAP)
    for turn in range(ITERS):
        packed = exchange(finish(exchange(parts), bf16))
        parts = round_sums(packed, members, own_owner, other, other_owner)
    packed = exchange(finish(exchange(parts), f32))
    theirs = assign(packed, other, other_owner)
    swapped = lax.ppermute(theirs, "c", SWAP)
    mine = assign(packed, members, own_owner)
    assignments = jnp.where(own_owner < OWN_LISTS, mine, swapped)
    place = lax.axis_index(("x", "z")) * 4
    held = lax.dynamic_slice_in_dim(packed, place, 4, axis=0)[:, :, :HALF_D]
    centers = held.reshape(2, 2, K, HALF_D).transpose(0, 2, 1, 3).reshape(2, K, D)
    return assignments, centers


def solution(mesh):
    fine = Mesh(mesh.devices.reshape(4, 4, 2, 4), ("x", "z", "c", "y"))
    every = ("x", "z", "c", "y")
    return jax.shard_map(
        local,
        mesh=fine,
        in_specs=(P(every, None), P(every, None), P(every)),
        out_specs=(P(None, every), P(("x", "z", "c"), None, None)),
        check_vma=False,
    )
```

```python
import jax
import jax.numpy as jnp
from jax import lax
from jax.experimental import pallas as pl
from jax.experimental.pallas import tpu as pltpu
from jax.sharding import Mesh, PartitionSpec as P

K = 8
D = 768
ITERS = 3
HALF_D = D // 2
LANES = 128
CHUNK = HALF_D + LANES
OWN_LISTS = 32
SEATS = 64
TILE = 512
UNROLL = 4
COPIES = 4
SEED_COPIES = 4
f32 = jnp.float32
bf16 = jnp.bfloat16


def lane_fold(block):
    total = block[:, :LANES]
    for at in range(LANES, block.shape[1], LANES):
        total = total + block[:, at : at + LANES]
    return total


def store_sums(out, acc, tot, base):
    for seat in range(SEATS):
        row, half = base + (seat // 2) * K, seat % 2
        out[seat, :, :HALF_D] = acc[row : row + K, half * HALF_D : (half + 1) * HALF_D]
        out[seat, :, HALF_D:] = tot[row : row + K, :]


def relative(names, core):
    away = ((names >> 1) & 1) ^ core
    return (names >> 2) * 2 + (names & 1) + OWN_LISTS * away


def start_copies(sources, buf, sems, copies):
    rows = sources[0].shape[0] // copies
    for number in range(len(sources) * copies):
        source = sources[number // copies].at[pl.ds(number % copies * rows, rows), :]
        pltpu.make_async_copy(source, buf.at[pl.ds(number * rows, rows), :], sems.at[number]).start()


def wait_copy(source, buf, sems, copies, number):
    rows = source.shape[0] // copies
    pltpu.make_async_copy(
        source.at[pl.ds(0, rows), :], buf.at[pl.ds(number * rows, rows), :], sems.at[number]
    ).wait()


def at_tile(tile):
    return pl.ds(pl.multiple_of(tile * TILE, TILE), TILE)


def seed_kernel(core, members, owner, seeds, mine, theirs, acc, tot, code, buf, sems):
    start_copies([members], buf, sems, SEED_COPIES)
    code[...] = relative(owner[...], core[0]) * K + seeds[...]
    acc[...] = jnp.zeros_like(acc)
    tot[...] = jnp.zeros_like(tot)
    groups = lax.broadcasted_iota(jnp.int32, (K, TILE), 0)
    unroll = buf.shape[0] // TILE // SEED_COPIES

    def work(turn, carry):
        wait_copy(members, buf, sems, SEED_COPIES, turn)
        for part in range(unroll):
            spot = at_tile(turn * unroll + part)
            shifted = jnp.broadcast_to(code[:, spot], (K, TILE)) - groups
            rows = []
            for name in range(2 * OWN_LISTS):
                hot = jnp.where(shifted == name * K, 1.0, 0.0).astype(f32)
                tot[name * K : (name + 1) * K, :] += lane_fold(hot)
                rows.append(hot)
            hots = jnp.concatenate(rows, axis=0).astype(bf16)
            acc[...] += jnp.dot(hots, buf[spot, :], preferred_element_type=f32)
        return carry

    lax.fori_loop(0, SEED_COPIES, work, 0)
    store_sums(mine, acc, tot, 0)
    store_sums(theirs, acc, tot, OWN_LISTS * K)


IN_VMEM = pl.BlockSpec(memory_space=pltpu.VMEM)
IN_SMEM = pl.BlockSpec(memory_space=pltpu.SMEM)
IN_PLACE = pl.BlockSpec(memory_space=pl.ANY)


def seed_sums(core, members, owner, seeds):
    part = jax.ShapeDtypeStruct((SEATS, K, CHUNK), f32)
    rows = members.shape[0]
    return pl.pallas_call(
        seed_kernel,
        in_specs=[IN_SMEM, IN_PLACE, IN_VMEM, IN_VMEM],
        out_specs=[IN_VMEM, IN_VMEM],
        out_shape=[part, part],
        scratch_shapes=[
            pltpu.VMEM((2 * OWN_LISTS * K, D), f32),
            pltpu.VMEM((2 * OWN_LISTS * K, LANES), f32),
            pltpu.VMEM((1, rows), jnp.int32),
            pltpu.VMEM((rows, D), bf16),
            pltpu.SemaphoreType.DMA((SEED_COPIES,)),
        ],
        name="seed_sums",
    )(core, members, owner, seeds)


def finish_kernel(parts, out):
    total = parts[0]
    for seat in range(1, SEATS):
        total = total + parts[seat]
    count = jnp.sum(total[:, HALF_D:], axis=1, keepdims=True)
    centers = total[:, :HALF_D] / (count + 1.0)
    norm = jnp.sum(centers * centers, axis=1, keepdims=True)
    lane = lax.broadcasted_iota(jnp.int32, (K, LANES), 1)
    norms = jnp.broadcast_to(norm, (K, LANES))
    if out.dtype == bf16:
        high = norms.astype(bf16).astype(f32)
        middle = (norms - high).astype(bf16).astype(f32)
        low = norms - high - middle
        tail = jnp.where(lane == 0, high, jnp.where(lane == 1, middle, jnp.where(lane == 2, low, 0.0)))
    else:
        tail = jnp.where(lane == 0, norms, 0.0)
    block = jnp.concatenate([centers, tail], axis=1).astype(out.dtype)
    for seat in range(SEATS):
        out[seat] = block


def finish(parts, dtype):
    return pl.pallas_call(
        finish_kernel,
        in_specs=[IN_VMEM],
        out_specs=IN_VMEM,
        out_shape=jax.ShapeDtypeStruct((SEATS, K, CHUNK), dtype),
        name="finish_" + jnp.dtype(dtype).name,
    )(parts)


def unpack_centers(packed, cen, nrm):
    for pair in range(OWN_LISTS // 2):
        for half in range(2):
            blocks = [packed[4 * pair + 2 * i + half].astype(f32) for i in range(2)]
            cen[pair * 16 : pair * 16 + 16, half * HALF_D : (half + 1) * HALF_D] = jnp.concatenate(
                [b[:, :HALF_D] for b in blocks], axis=0
            ).astype(bf16)
        for i in range(2):
            name = 2 * pair + i
            tails = packed[2 * name][:, HALF_D:].astype(f32) + packed[2 * name + 1][:, HALF_D:].astype(f32)
            nrm[name * K : (name + 1) * K, :] = jnp.broadcast_to(
                jnp.sum(tails, axis=1, keepdims=True), (K, LANES)
            )


def dots_of(tile, cen, buf):
    return lax.dot_general(
        cen[...], buf[at_tile(tile), :], (((1,), (1,)), ((), ())), preferred_element_type=f32
    )


def soft_weights(dots, slot, nrm, names):
    dot = jnp.zeros((K, TILE), f32)
    norm = jnp.zeros((K, TILE), f32)
    for name in range(OWN_LISTS):
        here = names == name
        rows = slice(name * K, (name + 1) * K)
        dot = jnp.where(here, dots[slot, rows, :], dot)
        norm = jnp.where(here, jnp.concatenate([nrm[rows, :]] * (TILE // LANES), axis=1), norm)
    logits = (2.0 * dot - norm) / 2.0
    exps = jnp.exp(logits - jnp.max(logits, axis=0, keepdims=True))
    return exps / jnp.sum(exps, axis=0, keepdims=True)


def both_owners(core, own_owner, other_owner, owners):
    rows = own_owner.shape[1]
    owners[:, :rows] = relative(own_owner[...], core)
    owners[:, rows:] = relative(other_owner[...], core)


def both_waits(own, buf, sems, turn):
    for number in range(2):
        wait_copy(own, buf, sems, COPIES, turn * 2 + number)


def round_kernel(
    core, packed, own, own_owner, other, other_owner, out, cen, nrm, acc, tot, owners, dots, buf, sems
):
    start_copies([own, other], buf, sems, COPIES)
    unpack_centers(packed, cen, nrm)
    both_owners(core[0], own_owner, other_owner, owners)
    acc[...] = jnp.zeros_like(acc)
    tot[...] = jnp.zeros_like(tot)

    def work(turn, carry):
        both_waits(own, buf, sems, turn)
        for part in range(UNROLL):
            dots[part] = dots_of(turn * UNROLL + part, cen, buf)
        for part in range(UNROLL):
            spot = at_tile(turn * UNROLL + part)
            names = jnp.broadcast_to(owners[:, spot], (K, TILE))
            weights = soft_weights(dots, part, nrm, names).astype(bf16).astype(f32)
            rows = []
            for name in range(OWN_LISTS):
                here = jnp.where(names == name, weights, 0.0)
                tot[name * K : (name + 1) * K, :] += lane_fold(here)
                rows.append(here)
            spread = jnp.concatenate(rows, axis=0).astype(bf16)
            acc[...] += jnp.dot(spread, buf[spot, :], preferred_element_type=f32)
        return carry

    lax.fori_loop(0, COPIES, work, 0)
    store_sums(out, acc, tot, 0)


def round_sums(core, packed, own, own_owner, other, other_owner):
    rows = 2 * own.shape[0]
    return pl.pallas_call(
        round_kernel,
        in_specs=[IN_SMEM, IN_VMEM, IN_PLACE, IN_VMEM, IN_PLACE, IN_VMEM],
        out_specs=IN_VMEM,
        out_shape=jax.ShapeDtypeStruct((SEATS, K, CHUNK), f32),
        scratch_shapes=[
            pltpu.VMEM((OWN_LISTS * K, D), bf16),
            pltpu.VMEM((OWN_LISTS * K, LANES), f32),
            pltpu.VMEM((OWN_LISTS * K, D), f32),
            pltpu.VMEM((OWN_LISTS * K, LANES), f32),
            pltpu.VMEM((1, rows), jnp.int32),
            pltpu.VMEM((UNROLL, OWN_LISTS * K, TILE), f32),
            pltpu.VMEM((rows, D), bf16),
            pltpu.SemaphoreType.DMA((2 * COPIES,)),
        ],
        name="round_sums",
    )(core, packed, own, own_owner, other, other_owner)


def assign_kernel(
    core, packed, own, own_owner, other, other_owner, out, held, cen, nrm, owners, dots, buf, sems
):
    start_copies([own, other], buf, sems, COPIES)
    unpack_centers(packed, cen, nrm)
    both_owners(core[0], own_owner, other_owner, owners)
    for name in range(2):
        for half in range(2):
            block = packed[core[1] + 2 * name + half]
            held[name, :, half * HALF_D : (half + 1) * HALF_D] = block[:, :HALF_D]

    def work(turn, carry):
        both_waits(own, buf, sems, turn)
        for part in range(UNROLL):
            dots[part] = dots_of(turn * UNROLL + part, cen, buf)
        for part in range(UNROLL):
            spot = at_tile(turn * UNROLL + part)
            names = jnp.broadcast_to(owners[:, spot], (K, TILE))
            out[:, spot] = jnp.where(names < OWN_LISTS, soft_weights(dots, part, nrm, names), 0.0)
        return carry

    lax.fori_loop(0, COPIES, work, 0)


def assign(core, packed, own, own_owner, other, other_owner):
    rows = 2 * own.shape[0]
    return pl.pallas_call(
        assign_kernel,
        in_specs=[IN_SMEM, IN_VMEM, IN_PLACE, IN_VMEM, IN_PLACE, IN_VMEM],
        out_specs=[IN_VMEM, IN_VMEM],
        out_shape=[jax.ShapeDtypeStruct((K, rows), f32), jax.ShapeDtypeStruct((2, K, D), f32)],
        scratch_shapes=[
            pltpu.VMEM((OWN_LISTS * K, D), bf16),
            pltpu.VMEM((OWN_LISTS * K, LANES), f32),
            pltpu.VMEM((1, rows), jnp.int32),
            pltpu.VMEM((UNROLL, OWN_LISTS * K, TILE), f32),
            pltpu.VMEM((rows, D), bf16),
            pltpu.SemaphoreType.DMA((2 * COPIES,)),
        ],
        name="assign",
    )(core, packed, own, own_owner, other, other_owner)


SWAP = [(0, 1), (1, 0)]
SEAT_AXES = ("x", "z", "y")


def local(members, owner, seed_label):
    place = jnp.stack([lax.axis_index("c"), lax.axis_index(("x", "z")) * 4]).astype(jnp.int32)
    owner = owner.reshape(1, -1)
    other = lax.ppermute(members, "c", SWAP)
    other_owner = lax.ppermute(owner, "c", SWAP)
    both = (members, owner, other, other_owner)

    def exchange(parts):
        return lax.all_to_all(parts, SEAT_AXES, split_axis=0, concat_axis=0, tiled=True)

    mine, theirs = seed_sums(place, members, owner, seed_label.reshape(1, -1))
    parts = mine + lax.ppermute(theirs, "c", SWAP)
    for turn in range(ITERS):
        packed = exchange(finish(exchange(parts), bf16))
        parts = round_sums(place, packed, *both)
    packed = exchange(finish(exchange(parts), f32))
    weights, centers = assign(place, packed, *both)
    rows = members.shape[0]
    swapped = lax.ppermute(weights[:, rows:], "c", SWAP)
    return weights[:, :rows] + swapped, centers


def solution(mesh):
    fine = Mesh(mesh.devices.reshape(4, 4, 2, 4), ("x", "z", "c", "y"))
    every = ("x", "z", "c", "y")
    return jax.shard_map(
        local,
        mesh=fine,
        in_specs=(P(every, None), P(every, None), P(every)),
        out_specs=(P(None, every), P(("x", "z", "c"), None, None)),
        check_vma=False,
    )
```

```python
import jax
import jax.numpy as jnp
from jax import lax
from jax.experimental import pallas as pl
from jax.experimental.pallas import tpu as pltpu
from jax.sharding import Mesh, PartitionSpec as P

K = 8
D = 768
ITERS = 3
HALF_D = D // 2
LANES = 128
CHUNK = HALF_D + LANES
OWN_LISTS = 32
SEATS = 64
TILE = 512
UNROLL = 4
COPIES = 4
SEED_COPIES = 4
f32 = jnp.float32
bf16 = jnp.bfloat16


def lane_fold(block):
    total = block[:, :LANES]
    for at in range(LANES, block.shape[1], LANES):
        total = total + block[:, at : at + LANES]
    return total


def store_sums(out, acc, tot, base):
    for seat in range(SEATS):
        row, half = base + (seat // 2) * K, seat % 2
        out[seat, :, :HALF_D] = acc[row : row + K, half * HALF_D : (half + 1) * HALF_D]
        out[seat, :, HALF_D:] = tot[row : row + K, :]


def relative(names, core):
    away = ((names >> 1) & 1) ^ core
    return (names >> 2) * 2 + (names & 1) + OWN_LISTS * away


def start_copies(sources, buf, sems, copies):
    rows = sources[0].shape[0] // copies
    for number in range(len(sources) * copies):
        source = sources[number // copies].at[pl.ds(number % copies * rows, rows), :]
        pltpu.make_async_copy(source, buf.at[pl.ds(number * rows, rows), :], sems.at[number]).start()


def wait_copy(source, buf, sems, copies, number):
    rows = source.shape[0] // copies
    pltpu.make_async_copy(
        source.at[pl.ds(0, rows), :], buf.at[pl.ds(number * rows, rows), :], sems.at[number]
    ).wait()


def at_tile(tile):
    return pl.ds(pl.multiple_of(tile * TILE, TILE), TILE)


def seed_kernel(core, members, owner, seeds, mine, theirs, acc, tot, code, buf, sems):
    start_copies([members], buf, sems, SEED_COPIES)
    code[...] = relative(owner[...], core[0]) * K + seeds[...]
    acc[...] = jnp.zeros_like(acc)
    tot[...] = jnp.zeros_like(tot)
    groups = lax.broadcasted_iota(jnp.int32, (K, TILE), 0)
    unroll = buf.shape[0] // TILE // SEED_COPIES

    def work(turn, carry):
        wait_copy(members, buf, sems, SEED_COPIES, turn)
        for part in range(unroll):
            spot = at_tile(turn * unroll + part)
            shifted = jnp.broadcast_to(code[:, spot], (K, TILE)) - groups
            rows = []
            for name in range(2 * OWN_LISTS):
                hot = jnp.where(shifted == name * K, 1.0, 0.0).astype(f32)
                tot[name * K : (name + 1) * K, :] += lane_fold(hot)
                rows.append(hot)
            hots = jnp.concatenate(rows, axis=0).astype(bf16)
            acc[...] += jnp.dot(hots, buf[spot, :], preferred_element_type=f32)
        return carry

    lax.fori_loop(0, SEED_COPIES, work, 0)
    store_sums(mine, acc, tot, 0)
    store_sums(theirs, acc, tot, OWN_LISTS * K)


IN_VMEM = pl.BlockSpec(memory_space=pltpu.VMEM)
IN_SMEM = pl.BlockSpec(memory_space=pltpu.SMEM)
IN_PLACE = pl.BlockSpec(memory_space=pltpu.HBM)


def seed_sums(core, members, owner, seeds):
    part = jax.ShapeDtypeStruct((SEATS, K, CHUNK), f32)
    rows = members.shape[0]
    return pl.pallas_call(
        seed_kernel,
        in_specs=[IN_SMEM, IN_PLACE, IN_VMEM, IN_VMEM],
        out_specs=[IN_VMEM, IN_VMEM],
        out_shape=[part, part],
        scratch_shapes=[
            pltpu.VMEM((2 * OWN_LISTS * K, D), f32),
            pltpu.VMEM((2 * OWN_LISTS * K, LANES), f32),
            pltpu.VMEM((1, rows), jnp.int32),
            pltpu.VMEM((rows, D), bf16),
            pltpu.SemaphoreType.DMA((SEED_COPIES,)),
        ],
        compiler_params=pltpu.CompilerParams(vmem_limit_bytes=59 << 20),
        name="seed_sums",
    )(core, members, owner, seeds)


def finish_kernel(parts, out, exact):
    total = parts[0]
    for seat in range(1, SEATS):
        total = total + parts[seat]
    count = jnp.sum(total[:, HALF_D:], axis=1, keepdims=True)
    centers = total[:, :HALF_D] / (count + 1.0)
    exact[...] = centers
    norm = jnp.sum(centers * centers, axis=1, keepdims=True)
    lane = lax.broadcasted_iota(jnp.int32, (K, LANES), 1)
    norms = jnp.broadcast_to(norm, (K, LANES))
    high = norms.astype(bf16).astype(f32)
    middle = (norms - high).astype(bf16).astype(f32)
    low = norms - high - middle
    tail = jnp.where(lane == 0, high, jnp.where(lane == 1, middle, jnp.where(lane == 2, low, 0.0)))
    block = jnp.concatenate([centers, tail], axis=1).astype(bf16)
    for seat in range(SEATS):
        out[seat] = block


def finish(parts):
    return pl.pallas_call(
        finish_kernel,
        in_specs=[IN_VMEM],
        out_specs=[IN_VMEM, IN_VMEM],
        out_shape=[
            jax.ShapeDtypeStruct((SEATS, K, CHUNK), bf16),
            jax.ShapeDtypeStruct((K, HALF_D), f32),
        ],
        compiler_params=pltpu.CompilerParams(vmem_limit_bytes=4 << 20),
        name="finish",
    )(parts)


def unpack_centers(packed, cen, nrm):
    for pair in range(OWN_LISTS // 2):
        for half in range(2):
            blocks = [packed[4 * pair + 2 * i + half].astype(f32) for i in range(2)]
            cen[pair * 16 : pair * 16 + 16, half * HALF_D : (half + 1) * HALF_D] = jnp.concatenate(
                [b[:, :HALF_D] for b in blocks], axis=0
            ).astype(bf16)
        for i in range(2):
            name = 2 * pair + i
            tails = packed[2 * name][:, HALF_D:].astype(f32) + packed[2 * name + 1][:, HALF_D:].astype(f32)
            nrm[name * K : (name + 1) * K, :] = jnp.broadcast_to(
                jnp.sum(tails, axis=1, keepdims=True), (K, LANES)
            )


def dots_of(tile, cen, buf):
    return lax.dot_general(
        cen[...], buf[at_tile(tile), :], (((1,), (1,)), ((), ())), preferred_element_type=f32
    )


def soft_weights(dots, slot, nrm, names):
    dot = jnp.zeros((K, TILE), f32)
    norm = jnp.zeros((K, TILE), f32)
    for name in range(OWN_LISTS):
        here = names == name
        rows = slice(name * K, (name + 1) * K)
        dot = jnp.where(here, dots[slot, rows, :], dot)
        norm = jnp.where(here, jnp.concatenate([nrm[rows, :]] * (TILE // LANES), axis=1), norm)
    logits = (2.0 * dot - norm) / 2.0
    exps = jnp.exp(logits - jnp.max(logits, axis=0, keepdims=True))
    return exps / jnp.sum(exps, axis=0, keepdims=True)


def both_owners(core, own_owner, other_owner, owners):
    rows = own_owner.shape[1]
    owners[:, :rows] = relative(own_owner[...], core)
    owners[:, rows:] = relative(other_owner[...], core)


def both_waits(own, buf, sems, turn):
    for number in range(2):
        wait_copy(own, buf, sems, COPIES, turn * 2 + number)


def round_kernel(
    core, packed, own, own_owner, other, other_owner, out, cen, nrm, acc, tot, owners, dots, buf, sems
):
    start_copies([own, other], buf, sems, COPIES)
    unpack_centers(packed, cen, nrm)
    both_owners(core[0], own_owner, other_owner, owners)
    acc[...] = jnp.zeros_like(acc)
    tot[...] = jnp.zeros_like(tot)

    def work(turn, carry):
        both_waits(own, buf, sems, turn)
        for part in range(UNROLL):
            dots[part] = dots_of(turn * UNROLL + part, cen, buf)
        for part in range(UNROLL):
            spot = at_tile(turn * UNROLL + part)
            names = jnp.broadcast_to(owners[:, spot], (K, TILE))
            weights = soft_weights(dots, part, nrm, names).astype(bf16).astype(f32)
            rows = []
            for name in range(OWN_LISTS):
                here = jnp.where(names == name, weights, 0.0)
                tot[name * K : (name + 1) * K, :] += lane_fold(here)
                rows.append(here)
            spread = jnp.concatenate(rows, axis=0).astype(bf16)
            acc[...] += jnp.dot(spread, buf[spot, :], preferred_element_type=f32)
        return carry

    lax.fori_loop(0, COPIES, work, 0)
    store_sums(out, acc, tot, 0)


def round_sums(core, packed, own, own_owner, other, other_owner):
    rows = 2 * own.shape[0]
    return pl.pallas_call(
        round_kernel,
        in_specs=[IN_SMEM, IN_VMEM, IN_PLACE, IN_VMEM, IN_PLACE, IN_VMEM],
        out_specs=IN_VMEM,
        out_shape=jax.ShapeDtypeStruct((SEATS, K, CHUNK), f32),
        scratch_shapes=[
            pltpu.VMEM((OWN_LISTS * K, D), bf16),
            pltpu.VMEM((OWN_LISTS * K, LANES), f32),
            pltpu.VMEM((OWN_LISTS * K, D), f32),
            pltpu.VMEM((OWN_LISTS * K, LANES), f32),
            pltpu.VMEM((1, rows), jnp.int32),
            pltpu.VMEM((UNROLL, OWN_LISTS * K, TILE), f32),
            pltpu.VMEM((rows, D), bf16),
            pltpu.SemaphoreType.DMA((2 * COPIES,)),
        ],
        compiler_params=pltpu.CompilerParams(vmem_limit_bytes=59 << 20),
        name="round_sums",
    )(core, packed, own, own_owner, other, other_owner)


def assign_kernel(
    core, packed, own, own_owner, other, other_owner, mine, near, far, wide,
    kept, given, held, cen, nrm, owners, dots, blocks, buf, sems,
):
    start_copies([own, other], buf, sems, COPIES)
    unpack_centers(packed, cen, nrm)
    both_owners(core[0], own_owner, other_owner, owners)
    for shift, block in enumerate((mine, near, far, wide)):
        blocks[shift] = block[...]
    for seat in range(4):
        held[seat // 2, :, seat % 2 * HALF_D : (seat % 2 + 1) * HALF_D] = blocks[(core[1] - seat) & 3]

    def work_on(out, first):
        def work(turn, carry):
            both_waits(own, buf, sems, turn + first)
            for part in range(UNROLL):
                dots[part] = dots_of((turn + first) * UNROLL + part, cen, buf)
            for part in range(UNROLL):
                names = jnp.broadcast_to(owners[:, at_tile((turn + first) * UNROLL + part)], (K, TILE))
                weights = soft_weights(dots, part, nrm, names)
                out[:, at_tile(turn * UNROLL + part)] = jnp.where(names < OWN_LISTS, weights, 0.0)
            return carry

        lax.fori_loop(0, COPIES // 2, work, 0)

    work_on(kept, 0)
    work_on(given, COPIES // 2)


def assign(core, packed, own, own_owner, other, other_owner, *blocks):
    rows = own.shape[0]
    part = jax.ShapeDtypeStruct((K, rows), f32)
    return pl.pallas_call(
        assign_kernel,
        in_specs=[IN_SMEM, IN_VMEM, IN_PLACE, IN_VMEM, IN_PLACE, IN_VMEM] + [IN_VMEM] * 4,
        out_specs=[IN_VMEM, IN_VMEM, IN_VMEM],
        out_shape=[part, part, jax.ShapeDtypeStruct((2, K, D), f32)],
        scratch_shapes=[
            pltpu.VMEM((OWN_LISTS * K, D), bf16),
            pltpu.VMEM((OWN_LISTS * K, LANES), f32),
            pltpu.VMEM((1, 2 * rows), jnp.int32),
            pltpu.VMEM((UNROLL, OWN_LISTS * K, TILE), f32),
            pltpu.VMEM((4, K, HALF_D), f32),
            pltpu.VMEM((2 * rows, D), bf16),
            pltpu.SemaphoreType.DMA((2 * COPIES,)),
        ],
        compiler_params=pltpu.CompilerParams(vmem_limit_bytes=59 << 20),
        name="assign",
    )(core, packed, own, own_owner, other, other_owner, *blocks)


SWAP = [(0, 1), (1, 0)]
SEAT_AXES = ("x", "z", "y")


def local(members, owner, seed_label):
    place = jnp.stack([lax.axis_index("c"), lax.axis_index("y")]).astype(jnp.int32)
    owner = owner.reshape(1, -1)
    other = lax.ppermute(members, "c", SWAP)
    other_owner = lax.ppermute(owner, "c", SWAP)
    both = (members, owner, other, other_owner)

    def exchange(parts):
        return lax.all_to_all(parts, SEAT_AXES, split_axis=0, concat_axis=0, tiled=True)

    mine, theirs = seed_sums(place, members, owner, seed_label.reshape(1, -1))
    parts = mine + lax.ppermute(theirs, "c", SWAP)
    for turn in range(ITERS):
        packed = exchange(finish(exchange(parts))[0])
        parts = round_sums(place, packed, *both)
    packed, exact = finish(exchange(parts))
    blocks = [exact] + [
        lax.ppermute(exact, "y", [(seat, (seat + shift) % 4) for seat in range(4)]) for shift in (1, 2, 3)
    ]
    kept, given, centers = assign(place, exchange(packed), *both, *blocks)
    return kept + lax.ppermute(given, "c", SWAP), centers


def solution(mesh):
    fine = Mesh(mesh.devices.reshape(4, 4, 2, 4), ("x", "z", "c", "y"))
    every = ("x", "z", "c", "y")
    return jax.shard_map(
        local,
        mesh=fine,
        in_specs=(P(every, None), P(every, None), P(every)),
        out_specs=(P(None, every), P(("x", "z", "c"), None, None)),
        check_vma=False,
    )
```

```python
import jax
import jax.numpy as jnp
from jax import lax
from jax.experimental import pallas as pl
from jax.experimental.pallas import tpu as pltpu
from jax.sharding import Mesh, PartitionSpec as P

K = 8
D = 768
ITERS = 3
HALF_D = D // 2
LANES = 128
CHUNK = HALF_D + LANES
OWN_LISTS = 32
SEATS = 64
TILE = 512
UNROLL = 4
COPIES = 4
SEED_COPIES = 4
f32 = jnp.float32
bf16 = jnp.bfloat16


def lane_fold(block):
    total = block[:, :LANES]
    for at in range(LANES, block.shape[1], LANES):
        total = total + block[:, at : at + LANES]
    return total


def store_sums(out, acc, tot, base):
    for seat in range(SEATS):
        row, half = base + (seat // 2) * K, seat % 2
        out[seat, :, :HALF_D] = acc[row : row + K, half * HALF_D : (half + 1) * HALF_D]
        out[seat, :, HALF_D:] = tot[row : row + K, :]


def relative(names, core):
    away = ((names >> 1) & 1) ^ core
    return (names >> 2) * 2 + (names & 1) + OWN_LISTS * away


def start_copies(sources, buf, sems, copies):
    rows = sources[0].shape[0] // copies
    for number in range(len(sources) * copies):
        source = sources[number // copies].at[pl.ds(number % copies * rows, rows), :]
        pltpu.make_async_copy(source, buf.at[pl.ds(number * rows, rows), :], sems.at[number]).start()


def wait_copy(source, buf, sems, copies, number):
    rows = source.shape[0] // copies
    pltpu.make_async_copy(
        source.at[pl.ds(0, rows), :], buf.at[pl.ds(number * rows, rows), :], sems.at[number]
    ).wait()


def at_tile(tile):
    return pl.ds(pl.multiple_of(tile * TILE, TILE), TILE)


def seed_kernel(core, members, owner, seeds, spare, mine, theirs, buf, acc, tot, code, sems):
    start_copies([members], buf, sems, SEED_COPIES)
    code[...] = relative(owner[...], core[0]) * K + seeds[...]
    acc[...] = jnp.zeros_like(acc)
    tot[...] = jnp.zeros_like(tot)
    groups = lax.broadcasted_iota(jnp.int32, (K, TILE), 0)
    unroll = buf.shape[0] // TILE // SEED_COPIES

    def work(turn, carry):
        wait_copy(members, buf, sems, SEED_COPIES, turn)
        for part in range(unroll):
            spot = at_tile(turn * unroll + part)
            shifted = jnp.broadcast_to(code[:, spot], (K, TILE)) - groups
            rows = []
            for name in range(2 * OWN_LISTS):
                hot = jnp.where(shifted == name * K, 1.0, 0.0).astype(f32)
                tot[name * K : (name + 1) * K, :] += lane_fold(hot)
                rows.append(hot)
            hots = jnp.concatenate(rows, axis=0).astype(bf16)
            acc[...] += jnp.dot(hots, buf[spot, :], preferred_element_type=f32)
        return carry

    lax.fori_loop(0, SEED_COPIES, work, 0)
    store_sums(mine, acc, tot, 0)
    store_sums(theirs, acc, tot, OWN_LISTS * K)


IN_VMEM = pl.BlockSpec(memory_space=pltpu.VMEM)
IN_SMEM = pl.BlockSpec(memory_space=pltpu.SMEM)
IN_PLACE = pl.BlockSpec(memory_space=pltpu.HBM)


def seed_sums(core, members, owner, seeds, other_owner):
    part = jax.ShapeDtypeStruct((SEATS, K, CHUNK), f32)
    rows = members.shape[0]
    return pl.pallas_call(
        seed_kernel,
        in_specs=[IN_SMEM, IN_PLACE, IN_VMEM, IN_VMEM, IN_PLACE],
        out_specs=[IN_VMEM, IN_VMEM, IN_VMEM],
        out_shape=[part, part, pltpu.VMEM((rows, D), bf16)],
        scratch_shapes=[
            pltpu.VMEM((2 * OWN_LISTS * K, D), f32),
            pltpu.VMEM((2 * OWN_LISTS * K, LANES), f32),
            pltpu.VMEM((1, rows), jnp.int32),
            pltpu.SemaphoreType.DMA((SEED_COPIES,)),
        ],
        compiler_params=pltpu.CompilerParams(vmem_limit_bytes=32 << 20),
        name="seed_sums",
    )(core, members, owner, seeds, other_owner)


def finish_kernel(parts, out, exact):
    total = parts[0]
    for seat in range(1, SEATS):
        total = total + parts[seat]
    count = jnp.sum(total[:, HALF_D:], axis=1, keepdims=True)
    centers = total[:, :HALF_D] / (count + 1.0)
    exact[...] = centers
    norm = jnp.sum(centers * centers, axis=1, keepdims=True)
    lane = lax.broadcasted_iota(jnp.int32, (K, LANES), 1)
    norms = jnp.broadcast_to(norm, (K, LANES))
    high = norms.astype(bf16).astype(f32)
    middle = (norms - high).astype(bf16).astype(f32)
    low = norms - high - middle
    tail = jnp.where(lane == 0, high, jnp.where(lane == 1, middle, jnp.where(lane == 2, low, 0.0)))
    block = jnp.concatenate([centers, tail], axis=1).astype(bf16)
    for seat in range(SEATS):
        out[seat] = block


def finish(parts):
    return pl.pallas_call(
        finish_kernel,
        in_specs=[IN_VMEM],
        out_specs=[IN_VMEM, IN_VMEM],
        out_shape=[
            jax.ShapeDtypeStruct((SEATS, K, CHUNK), bf16),
            jax.ShapeDtypeStruct((K, HALF_D), f32),
        ],
        compiler_params=pltpu.CompilerParams(vmem_limit_bytes=4 << 20),
        name="finish",
    )(parts)


def unpack_centers(packed, cen, nrm):
    for pair in range(OWN_LISTS // 2):
        for half in range(2):
            blocks = [packed[4 * pair + 2 * i + half].astype(f32) for i in range(2)]
            cen[pair * 16 : pair * 16 + 16, half * HALF_D : (half + 1) * HALF_D] = jnp.concatenate(
                [b[:, :HALF_D] for b in blocks], axis=0
            ).astype(bf16)
        for i in range(2):
            name = 2 * pair + i
            tails = packed[2 * name][:, HALF_D:].astype(f32) + packed[2 * name + 1][:, HALF_D:].astype(f32)
            nrm[name * K : (name + 1) * K, :] = jnp.broadcast_to(
                jnp.sum(tails, axis=1, keepdims=True), (K, LANES)
            )


def dots_of(tile, cen, members):
    return lax.dot_general(
        cen[...], members[at_tile(tile), :], (((1,), (1,)), ((), ())), preferred_element_type=f32
    )


def soft_weights(dots, slot, nrm, names):
    dot = jnp.zeros((K, TILE), f32)
    norm = jnp.zeros((K, TILE), f32)
    for name in range(OWN_LISTS):
        here = names == name
        rows = slice(name * K, (name + 1) * K)
        dot = jnp.where(here, dots[slot, rows, :], dot)
        norm = jnp.where(here, jnp.concatenate([nrm[rows, :]] * (TILE // LANES), axis=1), norm)
    logits = (2.0 * dot - norm) / 2.0
    exps = jnp.exp(logits - jnp.max(logits, axis=0, keepdims=True))
    return exps / jnp.sum(exps, axis=0, keepdims=True)


def both_owners(core, own_owner, other_owner, owners):
    rows = own_owner.shape[1]
    owners[:, :rows] = relative(own_owner[...], core)
    owners[:, rows:] = relative(other_owner[...], core)


def both_waits(own, buf, sems, turn):
    for number in range(2):
        wait_copy(own, buf, sems, COPIES, turn * 2 + number)


def add_group(members, owners, first, turn, cen, nrm, acc, tot, dots):
    for part in range(UNROLL):
        dots[part] = dots_of(turn * UNROLL + part, cen, members)
    for part in range(UNROLL):
        tile = turn * UNROLL + part
        names = jnp.broadcast_to(owners[:, at_tile(first + tile)], (K, TILE))
        weights = soft_weights(dots, part, nrm, names).astype(bf16).astype(f32)
        rows = []
        for name in range(OWN_LISTS):
            here = jnp.where(names == name, weights, 0.0)
            tot[name * K : (name + 1) * K, :] += lane_fold(here)
            rows.append(here)
        spread = jnp.concatenate(rows, axis=0).astype(bf16)
        acc[...] += jnp.dot(spread, members[at_tile(tile), :], preferred_element_type=f32)


def begin_round(core, packed, own_owner, other_owner, cen, nrm, acc, tot, owners):
    unpack_centers(packed, cen, nrm)
    both_owners(core[0], own_owner, other_owner, owners)
    acc[...] = jnp.zeros_like(acc)
    tot[...] = jnp.zeros_like(tot)


def first_kernel(
    core, packed, near, own_owner, other, other_owner, out, far, cen, nrm, acc, tot, owners, dots, sems
):
    start_copies([other], far, sems, COPIES)
    begin_round(core, packed, own_owner, other_owner, cen, nrm, acc, tot, owners)
    half = near.shape[0] // TILE
    groups = half // UNROLL

    def work_near(turn, carry):
        add_group(near, owners, 0, turn, cen, nrm, acc, tot, dots)
        return carry

    def work_far(turn, carry):
        for number in range(COPIES // groups):
            wait_copy(other, far, sems, COPIES, turn * (COPIES // groups) + number)
        add_group(far, owners, half, turn, cen, nrm, acc, tot, dots)
        return carry

    lax.fori_loop(0, groups, work_near, 0)
    lax.fori_loop(0, groups, work_far, 0)
    store_sums(out, acc, tot, 0)


def later_kernel(
    core, packed, near, own_owner, far, other_owner, out, cen, nrm, acc, tot, owners, dots
):
    begin_round(core, packed, own_owner, other_owner, cen, nrm, acc, tot, owners)
    half = near.shape[0] // TILE

    def work_near(turn, carry):
        add_group(near, owners, 0, turn, cen, nrm, acc, tot, dots)
        return carry

    def work_far(turn, carry):
        add_group(far, owners, half, turn, cen, nrm, acc, tot, dots)
        return carry

    lax.fori_loop(0, half // UNROLL, work_near, 0)
    lax.fori_loop(0, half // UNROLL, work_far, 0)
    store_sums(out, acc, tot, 0)


def round_scratch(rows):
    return [
        pltpu.VMEM((OWN_LISTS * K, D), bf16),
        pltpu.VMEM((OWN_LISTS * K, LANES), f32),
        pltpu.VMEM((OWN_LISTS * K, D), f32),
        pltpu.VMEM((OWN_LISTS * K, LANES), f32),
        pltpu.VMEM((1, 2 * rows), jnp.int32),
        pltpu.VMEM((UNROLL, OWN_LISTS * K, TILE), f32),
    ]


def first_round(core, packed, near, own_owner, other, other_owner):
    rows = near.shape[0]
    return pl.pallas_call(
        first_kernel,
        in_specs=[IN_SMEM, IN_VMEM, IN_VMEM, IN_VMEM, IN_PLACE, IN_VMEM],
        out_specs=[IN_VMEM, IN_VMEM],
        out_shape=[jax.ShapeDtypeStruct((SEATS, K, CHUNK), f32), pltpu.VMEM((rows, D), bf16)],
        scratch_shapes=round_scratch(rows) + [pltpu.SemaphoreType.DMA((COPIES,))],
        compiler_params=pltpu.CompilerParams(vmem_limit_bytes=24 << 20),
        name="first_round",
    )(core, packed, near, own_owner, other, other_owner)


def later_round(core, packed, near, own_owner, far, other_owner):
    return pl.pallas_call(
        later_kernel,
        in_specs=[IN_SMEM] + [IN_VMEM] * 5,
        out_specs=IN_VMEM,
        out_shape=jax.ShapeDtypeStruct((SEATS, K, CHUNK), f32),
        scratch_shapes=round_scratch(near.shape[0]),
        compiler_params=pltpu.CompilerParams(vmem_limit_bytes=24 << 20),
        name="later_round",
    )(core, packed, near, own_owner, far, other_owner)


def assign_kernel(
    core, packed, own, own_owner, other, other_owner, mine, near, far, wide,
    kept, given, held, cen, nrm, owners, dots, blocks, buf, sems,
):
    start_copies([own, other], buf, sems, COPIES)
    unpack_centers(packed, cen, nrm)
    both_owners(core[0], own_owner, other_owner, owners)
    for shift, block in enumerate((mine, near, far, wide)):
        blocks[shift] = block[...]
    for seat in range(4):
        held[seat // 2, :, seat % 2 * HALF_D : (seat % 2 + 1) * HALF_D] = blocks[(core[1] - seat) & 3]

    def work_on(out, first):
        def work(turn, carry):
            both_waits(own, buf, sems, turn + first)
            for part in range(UNROLL):
                dots[part] = dots_of((turn + first) * UNROLL + part, cen, buf)
            for part in range(UNROLL):
                names = jnp.broadcast_to(owners[:, at_tile((turn + first) * UNROLL + part)], (K, TILE))
                weights = soft_weights(dots, part, nrm, names)
                out[:, at_tile(turn * UNROLL + part)] = jnp.where(names < OWN_LISTS, weights, 0.0)
            return carry

        lax.fori_loop(0, COPIES // 2, work, 0)

    work_on(kept, 0)
    work_on(given, COPIES // 2)


def assign(core, packed, own, own_owner, other, other_owner, *blocks):
    rows = own.shape[0]
    part = jax.ShapeDtypeStruct((K, rows), f32)
    return pl.pallas_call(
        assign_kernel,
        in_specs=[IN_SMEM, IN_VMEM, IN_PLACE, IN_VMEM, IN_PLACE, IN_VMEM] + [IN_VMEM] * 4,
        out_specs=[IN_VMEM, IN_VMEM, IN_VMEM],
        out_shape=[part, part, jax.ShapeDtypeStruct((2, K, D), f32)],
        scratch_shapes=[
            pltpu.VMEM((OWN_LISTS * K, D), bf16),
            pltpu.VMEM((OWN_LISTS * K, LANES), f32),
            pltpu.VMEM((1, 2 * rows), jnp.int32),
            pltpu.VMEM((UNROLL, OWN_LISTS * K, TILE), f32),
            pltpu.VMEM((4, K, HALF_D), f32),
            pltpu.VMEM((2 * rows, D), bf16),
            pltpu.SemaphoreType.DMA((2 * COPIES,)),
        ],
        compiler_params=pltpu.CompilerParams(vmem_limit_bytes=32 << 20),
        name="assign",
    )(core, packed, own, own_owner, other, other_owner, *blocks)


SWAP = [(0, 1), (1, 0)]
SEAT_AXES = ("x", "z", "y")


def local(members, owner, seed_label):
    place = jnp.stack([lax.axis_index("c"), lax.axis_index("y")]).astype(jnp.int32)
    owner = owner.reshape(1, -1)
    other = lax.ppermute(members, "c", SWAP)
    other_owner = lax.ppermute(owner, "c", SWAP)
    members, other = (pltpu.with_memory_space_constraint(v, pltpu.HBM) for v in (members, other))

    def exchange(parts):
        return lax.all_to_all(parts, SEAT_AXES, split_axis=0, concat_axis=0, tiled=True)

    mine, theirs, near = seed_sums(place, members, owner, seed_label.reshape(1, -1), other_owner)
    parts = mine + lax.ppermute(theirs, "c", SWAP)
    packed = exchange(finish(exchange(parts))[0])
    parts, far = first_round(place, packed, near, owner, other, other_owner)
    for turn in range(ITERS - 1):
        packed = exchange(finish(exchange(parts))[0])
        parts = later_round(place, packed, near, owner, far, other_owner)
    packed, exact = finish(exchange(parts))
    blocks = [exact] + [
        lax.ppermute(exact, "y", [(seat, (seat + shift) % 4) for seat in range(4)]) for shift in (1, 2, 3)
    ]
    kept, given, centers = assign(place, exchange(packed), members, owner, other, other_owner, *blocks)
    return kept + lax.ppermute(given, "c", SWAP), centers


def solution(mesh):
    fine = Mesh(mesh.devices.reshape(4, 4, 2, 4), ("x", "z", "c", "y"))
    every = ("x", "z", "c", "y")
    return jax.shard_map(
        local,
        mesh=fine,
        in_specs=(P(every, None), P(every, None), P(every)),
        out_specs=(P(None, every), P(("x", "z", "c"), None, None)),
        check_vma=False,
    )
```

```python
import jax
import jax.numpy as jnp
from jax import lax
from jax.experimental import pallas as pl
from jax.experimental.pallas import tpu as pltpu
from jax.sharding import Mesh, PartitionSpec as P

K = 8
D = 768
ITERS = 3
HALF_D = D // 2
LANES = 128
CHUNK = HALF_D + LANES
OWN_LISTS = 32
SEATS = 64
TILE = 512
UNROLL = 8
COPIES = 4
SEED_COPIES = 4
f32 = jnp.float32
bf16 = jnp.bfloat16


def lane_fold(block):
    total = block[:, :LANES]
    for at in range(LANES, block.shape[1], LANES):
        total = total + block[:, at : at + LANES]
    return total


def store_sums(out, acc, tot, base):
    for seat in range(SEATS):
        row, half = base + (seat // 2) * K, seat % 2
        out[seat, :, :HALF_D] = acc[row : row + K, half * HALF_D : (half + 1) * HALF_D]
        out[seat, :, HALF_D:] = tot[row : row + K, :]


def relative(names, core):
    away = ((names >> 1) & 1) ^ core
    return (names >> 2) * 2 + (names & 1) + OWN_LISTS * away


def start_copies(sources, buf, sems, copies):
    rows = sources[0].shape[0] // copies
    for number in range(len(sources) * copies):
        source = sources[number // copies].at[pl.ds(number % copies * rows, rows), :]
        pltpu.make_async_copy(source, buf.at[pl.ds(number * rows, rows), :], sems.at[number]).start()


def wait_copy(source, buf, sems, copies, number):
    rows = source.shape[0] // copies
    pltpu.make_async_copy(
        source.at[pl.ds(0, rows), :], buf.at[pl.ds(number * rows, rows), :], sems.at[number]
    ).wait()


def at_tile(tile):
    return pl.ds(pl.multiple_of(tile * TILE, TILE), TILE)


def seed_kernel(core, members, owner, seeds, mine, theirs, ids, held, acc, tot, code, buf, sems, pair):
    start_copies([members], held, sems, SEED_COPIES)
    pltpu.make_async_copy(owner, ids, pair.at[0]).start()
    pltpu.make_async_copy(seeds, buf, pair.at[1]).start()
    acc[...] = jnp.zeros_like(acc)
    tot[...] = jnp.zeros_like(tot)
    pltpu.make_async_copy(owner, ids, pair.at[0]).wait()
    pltpu.make_async_copy(seeds, buf, pair.at[1]).wait()
    ids[...] = relative(ids[...], core[0])
    code[...] = ids[...] * K + buf[...]
    groups = lax.broadcasted_iota(jnp.int32, (K, TILE), 0)
    unroll = members.shape[0] // TILE // SEED_COPIES

    def work(turn, carry):
        wait_copy(members, held, sems, SEED_COPIES, turn)
        for part in range(unroll):
            spot = at_tile(turn * unroll + part)
            shifted = jnp.broadcast_to(code[:, spot], (K, TILE)) - groups
            rows = []
            for name in range(2 * OWN_LISTS):
                hot = jnp.where(shifted == name * K, 1.0, 0.0).astype(f32)
                tot[name * K : (name + 1) * K, :] += lane_fold(hot)
                rows.append(hot)
            hots = jnp.concatenate(rows, axis=0).astype(bf16)
            acc[...] += jnp.dot(hots, held[spot, :], preferred_element_type=f32)
        return carry

    lax.fori_loop(0, SEED_COPIES, work, 0)
    store_sums(mine, acc, tot, 0)
    store_sums(theirs, acc, tot, OWN_LISTS * K)


IN_VMEM = pl.BlockSpec(memory_space=pltpu.VMEM)
IN_SMEM = pl.BlockSpec(memory_space=pltpu.SMEM)
IN_PLACE = pl.BlockSpec(memory_space=pltpu.HBM)


def seed_sums(core, members, owner, seeds):
    part = jax.ShapeDtypeStruct((SEATS, K, CHUNK), f32)
    rows = members.shape[0]
    return pl.pallas_call(
        seed_kernel,
        in_specs=[IN_SMEM, IN_PLACE, IN_PLACE, IN_PLACE],
        out_specs=[IN_VMEM] * 4,
        out_shape=[
            part,
            part,
            jax.ShapeDtypeStruct((1, rows), jnp.int32),
            pltpu.VMEM((2 * rows, D), bf16),
        ],
        scratch_shapes=[
            pltpu.VMEM((2 * OWN_LISTS * K, D), f32),
            pltpu.VMEM((2 * OWN_LISTS * K, LANES), f32),
            pltpu.VMEM((1, rows), jnp.int32),
            pltpu.VMEM((1, rows), jnp.int32),
            pltpu.SemaphoreType.DMA((SEED_COPIES,)),
            pltpu.SemaphoreType.DMA((2,)),
        ],
        compiler_params=pltpu.CompilerParams(vmem_limit_bytes=24 << 20),
        name="seed_sums",
    )(core, members, owner, seeds)


def finish_kernel(parts, out, exact):
    total = parts[0]
    for seat in range(1, SEATS):
        total = total + parts[seat]
    count = jnp.sum(total[:, HALF_D:], axis=1, keepdims=True)
    centers = total[:, :HALF_D] / (count + 1.0)
    exact[...] = centers
    norm = jnp.sum(centers * centers, axis=1, keepdims=True)
    lane = lax.broadcasted_iota(jnp.int32, (K, LANES), 1)
    norms = jnp.broadcast_to(norm, (K, LANES))
    high = norms.astype(bf16).astype(f32)
    middle = (norms - high).astype(bf16).astype(f32)
    low = norms - high - middle
    tail = jnp.where(lane == 0, high, jnp.where(lane == 1, middle, jnp.where(lane == 2, low, 0.0)))
    block = jnp.concatenate([centers, tail], axis=1).astype(bf16)
    for seat in range(SEATS):
        out[seat] = block


def finish(parts):
    return pl.pallas_call(
        finish_kernel,
        in_specs=[IN_VMEM],
        out_specs=[IN_VMEM, IN_VMEM],
        out_shape=[
            jax.ShapeDtypeStruct((SEATS, K, CHUNK), bf16),
            jax.ShapeDtypeStruct((K, HALF_D), f32),
        ],
        compiler_params=pltpu.CompilerParams(vmem_limit_bytes=4 << 20),
        name="finish",
    )(parts)


def unpack_centers(packed, cen, nrm):
    for pair in range(OWN_LISTS // 2):
        for half in range(2):
            blocks = [packed[4 * pair + 2 * i + half].astype(f32) for i in range(2)]
            cen[pair * 16 : pair * 16 + 16, half * HALF_D : (half + 1) * HALF_D] = jnp.concatenate(
                [b[:, :HALF_D] for b in blocks], axis=0
            ).astype(bf16)
        for i in range(2):
            name = 2 * pair + i
            tails = packed[2 * name][:, HALF_D:].astype(f32) + packed[2 * name + 1][:, HALF_D:].astype(f32)
            nrm[name * K : (name + 1) * K, :] = jnp.broadcast_to(
                jnp.sum(tails, axis=1, keepdims=True), (K, LANES)
            )


def dots_of(tile, cen, members):
    return lax.dot_general(
        cen[...], members[at_tile(tile), :], (((1,), (1,)), ((), ())), preferred_element_type=f32
    )


def soft_weights(dots, slot, nrm, names, offset):
    dot = jnp.zeros((K, TILE), f32)
    norm = jnp.zeros((K, TILE), f32)
    for name in range(OWN_LISTS):
        here = names == name + offset
        rows = slice(name * K, (name + 1) * K)
        dot = jnp.where(here, dots[slot, rows, :], dot)
        norm = jnp.where(here, jnp.concatenate([nrm[rows, :]] * (TILE // LANES), axis=1), norm)
    logits = (2.0 * dot - norm) / 2.0
    exps = jnp.exp(logits - jnp.max(logits, axis=0, keepdims=True))
    return exps / jnp.sum(exps, axis=0, keepdims=True)


def add_members(near_ids, far_ids, held, ids, cen, nrm, acc, tot, dots, arrive):
    half = near_ids.shape[1]
    ids[:, :half] = near_ids[...]
    ids[:, half:] = far_ids[...] ^ OWN_LISTS
    acc[...] = jnp.zeros_like(acc)
    tot[...] = jnp.zeros_like(tot)

    def work(turn, carry):
        arrive(turn)
        for part in range(UNROLL):
            dots[part] = dots_of(turn * UNROLL + part, cen, held)
        for part in range(UNROLL):
            spot = at_tile(turn * UNROLL + part)
            names = jnp.broadcast_to(ids[:, spot], (K, TILE))
            weights = soft_weights(dots, part, nrm, names, 0).astype(bf16).astype(f32)
            rows = []
            for name in range(OWN_LISTS):
                here = jnp.where(names == name, weights, 0.0)
                tot[name * K : (name + 1) * K, :] += lane_fold(here)
                rows.append(here)
            spread = jnp.concatenate(rows, axis=0).astype(bf16)
            acc[...] += jnp.dot(spread, held[spot, :], preferred_element_type=f32)
        return carry

    lax.fori_loop(0, held.shape[0] // TILE // UNROLL, work, 0)


def first_kernel(packed, near_ids, other, far_ids, before, out, held, cen, nrm, acc, tot, ids, dots, sems):
    rows = other.shape[0] // COPIES

    def copy_of(number):
        place = pl.ds(number * rows, rows)
        target = pl.ds(other.shape[0] + number * rows, rows)
        return pltpu.make_async_copy(other.at[place, :], held.at[target, :], sems.at[number])

    for number in range(COPIES):
        copy_of(number).start()
    unpack_centers(packed, cen, nrm)

    def arrive(turn):
        @pl.when(turn == other.shape[0] // TILE // UNROLL)
        def _():
            for number in range(COPIES):
                copy_of(number).wait()

    add_members(near_ids, far_ids, held, ids, cen, nrm, acc, tot, dots, arrive)
    store_sums(out, acc, tot, 0)


def later_kernel(packed, near_ids, held, far_ids, out, cen, nrm, acc, tot, ids, dots):
    unpack_centers(packed, cen, nrm)
    add_members(near_ids, far_ids, held, ids, cen, nrm, acc, tot, dots, lambda turn: None)
    store_sums(out, acc, tot, 0)


def round_scratch(rows):
    return [
        pltpu.VMEM((OWN_LISTS * K, D), bf16),
        pltpu.VMEM((OWN_LISTS * K, LANES), f32),
        pltpu.VMEM((OWN_LISTS * K, D), f32),
        pltpu.VMEM((OWN_LISTS * K, LANES), f32),
        pltpu.VMEM((1, 2 * rows), jnp.int32),
        pltpu.VMEM((UNROLL, OWN_LISTS * K, TILE), f32),
    ]


def first_round(packed, near_ids, other, far_ids, held):
    rows = other.shape[0]
    return pl.pallas_call(
        first_kernel,
        in_specs=[IN_VMEM, IN_VMEM, IN_PLACE, IN_VMEM, IN_VMEM],
        out_specs=[IN_VMEM, IN_VMEM],
        out_shape=[jax.ShapeDtypeStruct((SEATS, K, CHUNK), f32), pltpu.VMEM((2 * rows, D), bf16)],
        input_output_aliases={4: 1},
        scratch_shapes=round_scratch(rows) + [pltpu.SemaphoreType.DMA((COPIES,))],
        compiler_params=pltpu.CompilerParams(vmem_limit_bytes=24 << 20),
        name="first_round",
    )(packed, near_ids, other, far_ids, held)


def later_round(packed, near_ids, held, far_ids):
    return pl.pallas_call(
        later_kernel,
        in_specs=[IN_VMEM] * 4,
        out_specs=IN_VMEM,
        out_shape=jax.ShapeDtypeStruct((SEATS, K, CHUNK), f32),
        scratch_shapes=round_scratch(held.shape[0] // 2),
        compiler_params=pltpu.CompilerParams(vmem_limit_bytes=24 << 20),
        name="later_round",
    )(packed, near_ids, held, far_ids)


def assign_kernel(
    place, packed, own, near_ids, other, far_ids, mine, near, far, wide,
    kept, given, held, cen, nrm, dots, blocks, buf, sems,
):
    start_copies([own, other], buf, sems, COPIES)
    unpack_centers(packed, cen, nrm)
    for shift, block in enumerate((mine, near, far, wide)):
        blocks[shift] = block[...]
    for seat in range(4):
        held[seat // 2, :, seat % 2 * HALF_D : (seat % 2 + 1) * HALF_D] = blocks[(place[1] - seat) & 3]
    half = own.shape[0] // TILE
    group = half // COPIES

    def work_on(out, ids, side):
        def work(turn, carry):
            wait_copy(own, buf, sems, COPIES, side * COPIES + turn)
            for part in range(group):
                dots[part] = dots_of(side * half + turn * group + part, cen, buf)
            for part in range(group):
                spot = at_tile(turn * group + part)
                names = jnp.broadcast_to(ids[:, spot], (K, TILE))
                weights = soft_weights(dots, part, nrm, names, side * OWN_LISTS)
                there = (names < OWN_LISTS) if side == 0 else (names >= OWN_LISTS)
                out[:, spot] = jnp.where(there, weights, 0.0)
            return carry

        lax.fori_loop(0, COPIES, work, 0)

    work_on(kept, near_ids, 0)
    work_on(given, far_ids, 1)


def assign(place, packed, own, near_ids, other, far_ids, *blocks):
    rows = own.shape[0]
    part = jax.ShapeDtypeStruct((K, rows), f32)
    return pl.pallas_call(
        assign_kernel,
        in_specs=[IN_SMEM, IN_VMEM, IN_PLACE, IN_VMEM, IN_PLACE, IN_VMEM] + [IN_VMEM] * 4,
        out_specs=[IN_VMEM, IN_VMEM, IN_VMEM],
        out_shape=[part, part, jax.ShapeDtypeStruct((2, K, D), f32)],
        scratch_shapes=[
            pltpu.VMEM((OWN_LISTS * K, D), bf16),
            pltpu.VMEM((OWN_LISTS * K, LANES), f32),
            pltpu.VMEM((rows // TILE // COPIES, OWN_LISTS * K, TILE), f32),
            pltpu.VMEM((4, K, HALF_D), f32),
            pltpu.VMEM((2 * rows, D), bf16),
            pltpu.SemaphoreType.DMA((2 * COPIES,)),
        ],
        compiler_params=pltpu.CompilerParams(vmem_limit_bytes=24 << 20),
        name="assign",
    )(place, packed, own, near_ids, other, far_ids, *blocks)


SWAP = [(0, 1), (1, 0)]
SEAT_AXES = ("x", "z", "y")


def local(members, owner, seed_label):
    place = jnp.stack([lax.axis_index("c"), lax.axis_index("y")]).astype(jnp.int32)
    swap = lambda value: lax.ppermute(value, "c", SWAP)
    members, other, owner, seeds = (
        pltpu.with_memory_space_constraint(v, pltpu.HBM)
        for v in (members, swap(members), owner.reshape(1, -1), seed_label.reshape(1, -1))
    )

    def exchange(parts):
        return lax.all_to_all(parts, SEAT_AXES, split_axis=0, concat_axis=0, tiled=True)

    mine, theirs, near_ids, held = seed_sums(place, members, owner, seeds)
    parts, far_ids = lax.optimization_barrier((mine + swap(theirs), swap(near_ids)))
    packed = exchange(finish(exchange(parts))[0])
    parts, held = first_round(packed, near_ids, other, far_ids, held)
    for turn in range(ITERS - 1):
        packed = exchange(finish(exchange(parts))[0])
        parts = later_round(packed, near_ids, held, far_ids)
    packed, exact = finish(exchange(parts))
    blocks = [exact] + [
        lax.ppermute(exact, "y", [(seat, (seat + shift) % 4) for seat in range(4)]) for shift in (1, 2, 3)
    ]
    kept, given, centers = assign(place, exchange(packed), members, near_ids, other, far_ids, *blocks)
    return kept + swap(given), centers


def solution(mesh):
    fine = Mesh(mesh.devices.reshape(4, 4, 2, 4), ("x", "z", "c", "y"))
    every = ("x", "z", "c", "y")
    return jax.shard_map(
        local,
        mesh=fine,
        in_specs=(P(every, None), P(every, None), P(every)),
        out_specs=(P(None, every), P(("x", "z", "c"), None, None)),
        check_vma=False,
    )
```

```python
import jax
import jax.numpy as jnp
from jax import lax
from jax.experimental import pallas as pl
from jax.experimental.pallas import tpu as pltpu
from jax.sharding import Mesh, PartitionSpec as P

K = 8
D = 768
ITERS = 3
HALF = K // 2
LANES = 128
CHUNK = D + LANES
OWN_LISTS = 32
SEATS = 64
TILE = 512
UNROLL = 8
COPIES = 4
SEED_COPIES = 4
f32 = jnp.float32
bf16 = jnp.bfloat16


def lane_fold(block):
    total = block[:, :LANES]
    for at in range(LANES, block.shape[1], LANES):
        total = total + block[:, at : at + LANES]
    return total


def store_sums(out, acc, tot, base):
    for seat in range(SEATS):
        row = base + seat * HALF
        out[seat, :, :D] = acc[row : row + HALF, :]
        out[seat, :, D:] = tot[row : row + HALF, :]


def relative(names, core):
    away = ((names >> 1) & 1) ^ core
    return (names >> 2) * 2 + (names & 1) + OWN_LISTS * away


def start_copies(sources, buf, sems, copies):
    rows = sources[0].shape[0] // copies
    for number in range(len(sources) * copies):
        source = sources[number // copies].at[pl.ds(number % copies * rows, rows), :]
        pltpu.make_async_copy(source, buf.at[pl.ds(number * rows, rows), :], sems.at[number]).start()


def wait_copy(source, buf, sems, copies, number):
    rows = source.shape[0] // copies
    pltpu.make_async_copy(
        source.at[pl.ds(0, rows), :], buf.at[pl.ds(number * rows, rows), :], sems.at[number]
    ).wait()


def at_tile(tile):
    return pl.ds(pl.multiple_of(tile * TILE, TILE), TILE)


def seed_kernel(core, members, owner, seeds, mine, theirs, ids, held, acc, tot, code, buf, sems, pair):
    start_copies([members], held, sems, SEED_COPIES)
    pltpu.make_async_copy(owner, ids, pair.at[0]).start()
    pltpu.make_async_copy(seeds, buf, pair.at[1]).start()
    acc[...] = jnp.zeros_like(acc)
    tot[...] = jnp.zeros_like(tot)
    pltpu.make_async_copy(owner, ids, pair.at[0]).wait()
    pltpu.make_async_copy(seeds, buf, pair.at[1]).wait()
    ids[...] = relative(ids[...], core[0])
    code[...] = ids[...] * K + buf[...]
    groups = lax.broadcasted_iota(jnp.int32, (K, TILE), 0)
    unroll = members.shape[0] // TILE // SEED_COPIES

    def work(turn, carry):
        wait_copy(members, held, sems, SEED_COPIES, turn)
        for part in range(unroll):
            spot = at_tile(turn * unroll + part)
            shifted = jnp.broadcast_to(code[:, spot], (K, TILE)) - groups
            rows = []
            for name in range(2 * OWN_LISTS):
                hot = jnp.where(shifted == name * K, 1.0, 0.0).astype(f32)
                tot[name * K : (name + 1) * K, :] += lane_fold(hot)
                rows.append(hot)
            hots = jnp.concatenate(rows, axis=0).astype(bf16)
            acc[...] += jnp.dot(hots, held[spot, :], preferred_element_type=f32)
        return carry

    lax.fori_loop(0, SEED_COPIES, work, 0)
    store_sums(mine, acc, tot, 0)
    store_sums(theirs, acc, tot, OWN_LISTS * K)


IN_VMEM = pl.BlockSpec(memory_space=pltpu.VMEM)
IN_SMEM = pl.BlockSpec(memory_space=pltpu.SMEM)
IN_PLACE = pl.BlockSpec(memory_space=pltpu.HBM)


def seed_sums(core, members, owner, seeds):
    part = jax.ShapeDtypeStruct((SEATS, HALF, CHUNK), f32)
    rows = members.shape[0]
    return pl.pallas_call(
        seed_kernel,
        in_specs=[IN_SMEM, IN_PLACE, IN_PLACE, IN_PLACE],
        out_specs=[IN_VMEM] * 4,
        out_shape=[
            part,
            part,
            jax.ShapeDtypeStruct((1, rows), jnp.int32),
            pltpu.VMEM((2 * rows, D), bf16),
        ],
        scratch_shapes=[
            pltpu.VMEM((2 * OWN_LISTS * K, D), f32),
            pltpu.VMEM((2 * OWN_LISTS * K, LANES), f32),
            pltpu.VMEM((1, rows), jnp.int32),
            pltpu.VMEM((1, rows), jnp.int32),
            pltpu.SemaphoreType.DMA((SEED_COPIES,)),
            pltpu.SemaphoreType.DMA((2,)),
        ],
        compiler_params=pltpu.CompilerParams(vmem_limit_bytes=24 << 20),
        name="seed_sums",
    )(core, members, owner, seeds)


def finish_kernel(parts, out, exact):
    total = parts[0]
    for seat in range(1, SEATS):
        total = total + parts[seat]
    count = jnp.sum(total[:, D:], axis=1, keepdims=True)
    centers = total[:, :D] / (count + 1.0)
    exact[...] = centers
    norm = jnp.sum(centers * centers, axis=1, keepdims=True)
    lane = lax.broadcasted_iota(jnp.int32, (HALF, LANES), 1)
    norms = jnp.broadcast_to(norm, (HALF, LANES))
    high = norms.astype(bf16).astype(f32)
    middle = (norms - high).astype(bf16).astype(f32)
    low = norms - high - middle
    tail = jnp.where(lane == 0, high, jnp.where(lane == 1, middle, jnp.where(lane == 2, low, 0.0)))
    block = jnp.concatenate([centers, tail], axis=1).astype(bf16)
    for seat in range(SEATS):
        out[seat] = block


def finish(parts):
    return pl.pallas_call(
        finish_kernel,
        in_specs=[IN_VMEM],
        out_specs=[IN_VMEM, IN_VMEM],
        out_shape=[
            jax.ShapeDtypeStruct((SEATS, HALF, CHUNK), bf16),
            jax.ShapeDtypeStruct((HALF, D), f32),
        ],
        compiler_params=pltpu.CompilerParams(vmem_limit_bytes=4 << 20),
        name="finish",
    )(parts)


def unpack_centers(packed, cen, nrm):
    for group in range(OWN_LISTS // 2):
        blocks = [packed[4 * group + part].astype(f32) for part in range(4)]
        rows = slice(group * 2 * K, (group + 1) * 2 * K)
        cen[rows, :] = jnp.concatenate([b[:, :D] for b in blocks], axis=0).astype(bf16)
        tails = jnp.concatenate([b[:, D:] for b in blocks], axis=0)
        nrm[rows, :] = jnp.broadcast_to(jnp.sum(tails, axis=1, keepdims=True), (2 * K, LANES))


def dots_of(tile, cen, members):
    return lax.dot_general(
        cen[...], members[at_tile(tile), :], (((1,), (1,)), ((), ())), preferred_element_type=f32
    )


def soft_weights(dots, slot, nrm, names, offset):
    dot = jnp.zeros((K, TILE), f32)
    norm = jnp.zeros((K, TILE), f32)
    for name in range(OWN_LISTS):
        here = names == name + offset
        rows = slice(name * K, (name + 1) * K)
        dot = jnp.where(here, dots[slot, rows, :], dot)
        norm = jnp.where(here, jnp.concatenate([nrm[rows, :]] * (TILE // LANES), axis=1), norm)
    logits = (2.0 * dot - norm) / 2.0
    exps = jnp.exp(logits - jnp.max(logits, axis=0, keepdims=True))
    return exps / jnp.sum(exps, axis=0, keepdims=True)


def add_members(near_ids, far_ids, held, ids, cen, nrm, acc, tot, dots, arrive):
    half = near_ids.shape[1]
    ids[:, :half] = near_ids[...]
    ids[:, half:] = far_ids[...] ^ OWN_LISTS
    acc[...] = jnp.zeros_like(acc)
    tot[...] = jnp.zeros_like(tot)

    def work(turn, carry):
        arrive(turn)
        for part in range(UNROLL):
            dots[part] = dots_of(turn * UNROLL + part, cen, held)
        for part in range(UNROLL):
            spot = at_tile(turn * UNROLL + part)
            names = jnp.broadcast_to(ids[:, spot], (K, TILE))
            weights = soft_weights(dots, part, nrm, names, 0).astype(bf16).astype(f32)
            rows = []
            for name in range(OWN_LISTS):
                here = jnp.where(names == name, weights, 0.0)
                tot[name * K : (name + 1) * K, :] += lane_fold(here)
                rows.append(here)
            spread = jnp.concatenate(rows, axis=0).astype(bf16)
            acc[...] += jnp.dot(spread, held[spot, :], preferred_element_type=f32)
        return carry

    lax.fori_loop(0, held.shape[0] // TILE // UNROLL, work, 0)


def first_kernel(packed, near_ids, other, far_ids, before, out, held, cen, nrm, acc, tot, ids, dots, sems):
    rows = other.shape[0] // COPIES

    def copy_of(number):
        place = pl.ds(number * rows, rows)
        target = pl.ds(other.shape[0] + number * rows, rows)
        return pltpu.make_async_copy(other.at[place, :], held.at[target, :], sems.at[number])

    for number in range(COPIES):
        copy_of(number).start()
    unpack_centers(packed, cen, nrm)

    def arrive(turn):
        @pl.when(turn == other.shape[0] // TILE // UNROLL)
        def _():
            for number in range(COPIES):
                copy_of(number).wait()

    add_members(near_ids, far_ids, held, ids, cen, nrm, acc, tot, dots, arrive)
    store_sums(out, acc, tot, 0)


def later_kernel(packed, near_ids, held, far_ids, out, cen, nrm, acc, tot, ids, dots):
    unpack_centers(packed, cen, nrm)
    add_members(near_ids, far_ids, held, ids, cen, nrm, acc, tot, dots, lambda turn: None)
    store_sums(out, acc, tot, 0)


def round_scratch(rows):
    return [
        pltpu.VMEM((OWN_LISTS * K, D), bf16),
        pltpu.VMEM((OWN_LISTS * K, LANES), f32),
        pltpu.VMEM((OWN_LISTS * K, D), f32),
        pltpu.VMEM((OWN_LISTS * K, LANES), f32),
        pltpu.VMEM((1, 2 * rows), jnp.int32),
        pltpu.VMEM((UNROLL, OWN_LISTS * K, TILE), f32),
    ]


def first_round(packed, near_ids, other, far_ids, held):
    rows = other.shape[0]
    return pl.pallas_call(
        first_kernel,
        in_specs=[IN_VMEM, IN_VMEM, IN_PLACE, IN_VMEM, IN_VMEM],
        out_specs=[IN_VMEM, IN_VMEM],
        out_shape=[jax.ShapeDtypeStruct((SEATS, HALF, CHUNK), f32), pltpu.VMEM((2 * rows, D), bf16)],
        input_output_aliases={4: 1},
        scratch_shapes=round_scratch(rows) + [pltpu.SemaphoreType.DMA((COPIES,))],
        compiler_params=pltpu.CompilerParams(vmem_limit_bytes=24 << 20),
        name="first_round",
    )(packed, near_ids, other, far_ids, held)


def later_round(packed, near_ids, held, far_ids):
    return pl.pallas_call(
        later_kernel,
        in_specs=[IN_VMEM] * 4,
        out_specs=IN_VMEM,
        out_shape=jax.ShapeDtypeStruct((SEATS, HALF, CHUNK), f32),
        scratch_shapes=round_scratch(held.shape[0] // 2),
        compiler_params=pltpu.CompilerParams(vmem_limit_bytes=24 << 20),
        name="later_round",
    )(packed, near_ids, held, far_ids)


def assign_kernel(
    place, packed, own, near_ids, other, far_ids, mine, near, far, wide,
    kept, given, held, cen, nrm, dots, blocks, buf, sems,
):
    start_copies([own, other], buf, sems, COPIES)
    unpack_centers(packed, cen, nrm)
    for shift, block in enumerate((mine, near, far, wide)):
        blocks[shift] = block[...]
    for seat in range(4):
        held[seat // 2, seat % 2 * HALF : (seat % 2 + 1) * HALF, :] = blocks[(place[1] - seat) & 3]
    half = own.shape[0] // TILE
    group = half // COPIES

    def work_on(out, ids, side):
        def work(turn, carry):
            wait_copy(own, buf, sems, COPIES, side * COPIES + turn)
            for part in range(group):
                dots[part] = dots_of(side * half + turn * group + part, cen, buf)
            for part in range(group):
                spot = at_tile(turn * group + part)
                names = jnp.broadcast_to(ids[:, spot], (K, TILE))
                weights = soft_weights(dots, part, nrm, names, side * OWN_LISTS)
                there = (names < OWN_LISTS) if side == 0 else (names >= OWN_LISTS)
                out[:, spot] = jnp.where(there, weights, 0.0)
            return carry

        lax.fori_loop(0, COPIES, work, 0)

    work_on(kept, near_ids, 0)
    work_on(given, far_ids, 1)


def assign(place, packed, own, near_ids, other, far_ids, *blocks):
    rows = own.shape[0]
    part = jax.ShapeDtypeStruct((K, rows), f32)
    return pl.pallas_call(
        assign_kernel,
        in_specs=[IN_SMEM, IN_VMEM, IN_PLACE, IN_VMEM, IN_PLACE, IN_VMEM] + [IN_VMEM] * 4,
        out_specs=[IN_VMEM, IN_VMEM, IN_VMEM],
        out_shape=[part, part, jax.ShapeDtypeStruct((2, K, D), f32)],
        scratch_shapes=[
            pltpu.VMEM((OWN_LISTS * K, D), bf16),
            pltpu.VMEM((OWN_LISTS * K, LANES), f32),
            pltpu.VMEM((rows // TILE // COPIES, OWN_LISTS * K, TILE), f32),
            pltpu.VMEM((4, HALF, D), f32),
            pltpu.VMEM((2 * rows, D), bf16),
            pltpu.SemaphoreType.DMA((2 * COPIES,)),
        ],
        compiler_params=pltpu.CompilerParams(vmem_limit_bytes=24 << 20),
        name="assign",
    )(place, packed, own, near_ids, other, far_ids, *blocks)


SWAP = [(0, 1), (1, 0)]
SEAT_AXES = ("x", "z", "y")


def local(members, owner, seed_label):
    place = jnp.stack([lax.axis_index("c"), lax.axis_index("y")]).astype(jnp.int32)
    swap = lambda value: lax.ppermute(value, "c", SWAP)
    members, other, owner, seeds = (
        pltpu.with_memory_space_constraint(v, pltpu.HBM)
        for v in (members, swap(members), owner.reshape(1, -1), seed_label.reshape(1, -1))
    )

    def exchange(parts):
        return lax.all_to_all(parts, SEAT_AXES, split_axis=0, concat_axis=0, tiled=True)

    mine, theirs, near_ids, held = seed_sums(place, members, owner, seeds)
    parts, far_ids = lax.optimization_barrier((mine + swap(theirs), swap(near_ids)))
    packed = exchange(finish(exchange(parts))[0])
    parts, held = first_round(packed, near_ids, other, far_ids, held)
    for turn in range(ITERS - 1):
        packed = exchange(finish(exchange(parts))[0])
        parts = later_round(packed, near_ids, held, far_ids)
    packed, exact = finish(exchange(parts))
    blocks = [exact] + [
        lax.ppermute(exact, "y", [(seat, (seat + shift) % 4) for seat in range(4)]) for shift in (1, 2, 3)
    ]
    kept, given, centers = assign(place, exchange(packed), members, near_ids, other, far_ids, *blocks)
    return kept + swap(given), centers


def solution(mesh):
    fine = Mesh(mesh.devices.reshape(4, 4, 2, 4), ("x", "z", "c", "y"))
    every = ("x", "z", "c", "y")
    return jax.shard_map(
        local,
        mesh=fine,
        in_specs=(P(every, None), P(every, None), P(every)),
        out_specs=(P(None, every), P(("x", "z", "c"), None, None)),
        check_vma=False,
    )
```

```python
import jax
import jax.numpy as jnp
from jax import lax
from jax.experimental import pallas as pl
from jax.experimental.pallas import tpu as pltpu
from jax.sharding import Mesh, PartitionSpec as P

K = 8
D = 768
ITERS = 3
HALF = K // 2
LANES = 128
CHUNK = D + LANES
OWN_LISTS = 32
SEATS = 64
TILE = 512
UNROLL = 8
COPIES = 4
SEED_COPIES = 4
f32 = jnp.float32
bf16 = jnp.bfloat16


def lane_fold(block):
    total = block[:, :LANES]
    for at in range(LANES, block.shape[1], LANES):
        total = total + block[:, at : at + LANES]
    return total


def store_sums(out, acc, tot, base):
    for seat in range(SEATS):
        row = base + seat * HALF
        out[seat, :, :D] = acc[row : row + HALF, :]
        out[seat, :, D:] = tot[row : row + HALF, :]


def relative(names, core):
    away = ((names >> 1) & 1) ^ core
    return (names >> 2) * 2 + (names & 1) + OWN_LISTS * away


def start_copies(sources, buf, sems, copies):
    rows = sources[0].shape[0] // copies
    for number in range(len(sources) * copies):
        source = sources[number // copies].at[pl.ds(number % copies * rows, rows), :]
        pltpu.make_async_copy(source, buf.at[pl.ds(number * rows, rows), :], sems.at[number]).start()


def wait_copy(source, buf, sems, copies, number):
    rows = source.shape[0] // copies
    pltpu.make_async_copy(
        source.at[pl.ds(0, rows), :], buf.at[pl.ds(number * rows, rows), :], sems.at[number]
    ).wait()


def at_tile(tile):
    return pl.ds(pl.multiple_of(tile * TILE, TILE), TILE)


def add_seeds(code, held, acc, tot, base, tile):
    spot = at_tile(tile)
    groups = lax.broadcasted_iota(jnp.int32, (K, TILE), 0)
    shifted = jnp.broadcast_to(code[:, spot], (K, TILE)) - groups
    rows = []
    for name in range(OWN_LISTS):
        hot = jnp.where(shifted == base + name * K, 1.0, 0.0).astype(f32)
        tot[name * K : (name + 1) * K, :] += lane_fold(hot)
        rows.append(hot)
    hots = jnp.concatenate(rows, axis=0).astype(bf16)
    acc[...] += jnp.dot(hots, held[spot, :], preferred_element_type=f32)


def seed_away_kernel(core, members, owner, seeds, theirs, ids, code, held, acc, tot, buf, sems, pair):
    start_copies([members], held, sems, SEED_COPIES)
    pltpu.make_async_copy(owner, ids, pair.at[0]).start()
    pltpu.make_async_copy(seeds, buf, pair.at[1]).start()
    acc[...] = jnp.zeros_like(acc)
    tot[...] = jnp.zeros_like(tot)
    pltpu.make_async_copy(owner, ids, pair.at[0]).wait()
    pltpu.make_async_copy(seeds, buf, pair.at[1]).wait()
    ids[...] = relative(ids[...], core[0])
    code[...] = ids[...] * K + buf[...]
    unroll = members.shape[0] // TILE // SEED_COPIES

    def work(turn, carry):
        wait_copy(members, held, sems, SEED_COPIES, turn)
        for part in range(unroll):
            add_seeds(code, held, acc, tot, OWN_LISTS * K, turn * unroll + part)
        return carry

    lax.fori_loop(0, SEED_COPIES, work, 0)
    store_sums(theirs, acc, tot, 0)


def seed_own_kernel(code, held, mine, acc, tot):
    acc[...] = jnp.zeros_like(acc)
    tot[...] = jnp.zeros_like(tot)
    for tile in range(code.shape[1] // TILE):
        add_seeds(code, held, acc, tot, 0, tile)
    store_sums(mine, acc, tot, 0)


IN_VMEM = pl.BlockSpec(memory_space=pltpu.VMEM)
IN_SMEM = pl.BlockSpec(memory_space=pltpu.SMEM)
IN_PLACE = pl.BlockSpec(memory_space=pltpu.HBM)


PART = jax.ShapeDtypeStruct((SEATS, HALF, CHUNK), f32)
SUM_SCRATCH = [pltpu.VMEM((OWN_LISTS * K, D), f32), pltpu.VMEM((OWN_LISTS * K, LANES), f32)]
ROOM = pltpu.CompilerParams(vmem_limit_bytes=24 << 20)


def seed_away(core, members, owner, seeds):
    rows = members.shape[0]
    names = jax.ShapeDtypeStruct((1, rows), jnp.int32)
    return pl.pallas_call(
        seed_away_kernel,
        in_specs=[IN_SMEM, IN_PLACE, IN_PLACE, IN_PLACE],
        out_specs=[IN_VMEM] * 4,
        out_shape=[PART, names, names, pltpu.VMEM((2 * rows, D), bf16)],
        scratch_shapes=SUM_SCRATCH
        + [
            pltpu.VMEM((1, rows), jnp.int32),
            pltpu.SemaphoreType.DMA((SEED_COPIES,)),
            pltpu.SemaphoreType.DMA((2,)),
        ],
        compiler_params=ROOM,
        name="seed_away",
    )(core, members, owner, seeds)


def seed_own(code, held):
    return pl.pallas_call(
        seed_own_kernel,
        in_specs=[IN_VMEM, IN_VMEM],
        out_specs=IN_VMEM,
        out_shape=PART,
        scratch_shapes=SUM_SCRATCH,
        compiler_params=ROOM,
        name="seed_own",
    )(code, held)


def finish_kernel(parts, out, exact):
    total = parts[0]
    for seat in range(1, SEATS):
        total = total + parts[seat]
    count = jnp.sum(total[:, D:], axis=1, keepdims=True)
    centers = total[:, :D] / (count + 1.0)
    exact[...] = centers
    norm = jnp.sum(centers * centers, axis=1, keepdims=True)
    lane = lax.broadcasted_iota(jnp.int32, (HALF, LANES), 1)
    norms = jnp.broadcast_to(norm, (HALF, LANES))
    high = norms.astype(bf16).astype(f32)
    middle = (norms - high).astype(bf16).astype(f32)
    low = norms - high - middle
    tail = jnp.where(lane == 0, high, jnp.where(lane == 1, middle, jnp.where(lane == 2, low, 0.0)))
    block = jnp.concatenate([centers, tail], axis=1).astype(bf16)
    for seat in range(SEATS):
        out[seat] = block


def finish(parts):
    return pl.pallas_call(
        finish_kernel,
        in_specs=[IN_VMEM],
        out_specs=[IN_VMEM, IN_VMEM],
        out_shape=[
            jax.ShapeDtypeStruct((SEATS, HALF, CHUNK), bf16),
            jax.ShapeDtypeStruct((HALF, D), f32),
        ],
        compiler_params=pltpu.CompilerParams(vmem_limit_bytes=4 << 20),
        name="finish",
    )(parts)


def unpack_centers(packed, cen, nrm):
    for group in range(OWN_LISTS // 2):
        blocks = [packed[4 * group + part].astype(f32) for part in range(4)]
        rows = slice(group * 2 * K, (group + 1) * 2 * K)
        cen[rows, :] = jnp.concatenate([b[:, :D] for b in blocks], axis=0).astype(bf16)
        tails = jnp.concatenate([b[:, D:] for b in blocks], axis=0)
        nrm[rows, :] = jnp.broadcast_to(jnp.sum(tails, axis=1, keepdims=True), (2 * K, LANES))


def dots_of(tile, cen, members):
    return lax.dot_general(
        cen[...], members[at_tile(tile), :], (((1,), (1,)), ((), ())), preferred_element_type=f32
    )


def soft_weights(dots, slot, nrm, names, offset):
    dot = jnp.zeros((K, TILE), f32)
    norm = jnp.zeros((K, TILE), f32)
    for name in range(OWN_LISTS):
        here = names == name + offset
        rows = slice(name * K, (name + 1) * K)
        dot = jnp.where(here, dots[slot, rows, :], dot)
        norm = jnp.where(here, jnp.concatenate([nrm[rows, :]] * (TILE // LANES), axis=1), norm)
    logits = (2.0 * dot - norm) / 2.0
    exps = jnp.exp(logits - jnp.max(logits, axis=0, keepdims=True))
    return exps / jnp.sum(exps, axis=0, keepdims=True)


def add_members(near_ids, far_ids, held, ids, cen, nrm, acc, tot, dots, arrive):
    half = near_ids.shape[1]
    ids[:, :half] = near_ids[...]
    ids[:, half:] = far_ids[...] ^ OWN_LISTS
    acc[...] = jnp.zeros_like(acc)
    tot[...] = jnp.zeros_like(tot)

    def work(turn, carry):
        arrive(turn)
        for part in range(UNROLL):
            dots[part] = dots_of(turn * UNROLL + part, cen, held)
        for part in range(UNROLL):
            spot = at_tile(turn * UNROLL + part)
            names = jnp.broadcast_to(ids[:, spot], (K, TILE))
            weights = soft_weights(dots, part, nrm, names, 0).astype(bf16).astype(f32)
            rows = []
            for name in range(OWN_LISTS):
                here = jnp.where(names == name, weights, 0.0)
                tot[name * K : (name + 1) * K, :] += lane_fold(here)
                rows.append(here)
            spread = jnp.concatenate(rows, axis=0).astype(bf16)
            acc[...] += jnp.dot(spread, held[spot, :], preferred_element_type=f32)
        return carry

    lax.fori_loop(0, held.shape[0] // TILE // UNROLL, work, 0)


def first_kernel(packed, near_ids, other, far_ids, before, out, held, cen, nrm, acc, tot, ids, dots, sems):
    rows = other.shape[0] // COPIES

    def copy_of(number):
        place = pl.ds(number * rows, rows)
        target = pl.ds(other.shape[0] + number * rows, rows)
        return pltpu.make_async_copy(other.at[place, :], held.at[target, :], sems.at[number])

    for number in range(COPIES):
        copy_of(number).start()
    unpack_centers(packed, cen, nrm)

    def arrive(turn):
        @pl.when(turn == other.shape[0] // TILE // UNROLL)
        def _():
            for number in range(COPIES):
                copy_of(number).wait()

    add_members(near_ids, far_ids, held, ids, cen, nrm, acc, tot, dots, arrive)
    store_sums(out, acc, tot, 0)


def later_kernel(packed, near_ids, held, far_ids, out, cen, nrm, acc, tot, ids, dots):
    unpack_centers(packed, cen, nrm)
    add_members(near_ids, far_ids, held, ids, cen, nrm, acc, tot, dots, lambda turn: None)
    store_sums(out, acc, tot, 0)


def round_scratch(rows):
    return [
        pltpu.VMEM((OWN_LISTS * K, D), bf16),
        pltpu.VMEM((OWN_LISTS * K, LANES), f32),
        pltpu.VMEM((OWN_LISTS * K, D), f32),
        pltpu.VMEM((OWN_LISTS * K, LANES), f32),
        pltpu.VMEM((1, 2 * rows), jnp.int32),
        pltpu.VMEM((UNROLL, OWN_LISTS * K, TILE), f32),
    ]


def first_round(packed, near_ids, other, far_ids, held):
    rows = other.shape[0]
    return pl.pallas_call(
        first_kernel,
        in_specs=[IN_VMEM, IN_VMEM, IN_PLACE, IN_VMEM, IN_VMEM],
        out_specs=[IN_VMEM, IN_VMEM],
        out_shape=[jax.ShapeDtypeStruct((SEATS, HALF, CHUNK), f32), pltpu.VMEM((2 * rows, D), bf16)],
        input_output_aliases={4: 1},
        scratch_shapes=round_scratch(rows) + [pltpu.SemaphoreType.DMA((COPIES,))],
        compiler_params=pltpu.CompilerParams(vmem_limit_bytes=24 << 20),
        name="first_round",
    )(packed, near_ids, other, far_ids, held)


def later_round(packed, near_ids, held, far_ids):
    return pl.pallas_call(
        later_kernel,
        in_specs=[IN_VMEM] * 4,
        out_specs=IN_VMEM,
        out_shape=jax.ShapeDtypeStruct((SEATS, HALF, CHUNK), f32),
        scratch_shapes=round_scratch(held.shape[0] // 2),
        compiler_params=pltpu.CompilerParams(vmem_limit_bytes=24 << 20),
        name="later_round",
    )(packed, near_ids, held, far_ids)


def assign_members(packed, members, ids, out, cen, nrm, dots, buf, sems, side):
    start_copies([members], buf, sems, COPIES)
    unpack_centers(packed, cen, nrm)
    group = members.shape[0] // TILE // COPIES

    def work(turn, carry):
        wait_copy(members, buf, sems, COPIES, turn)
        for part in range(group):
            dots[part] = dots_of(turn * group + part, cen, buf)
        for part in range(group):
            spot = at_tile(turn * group + part)
            names = jnp.broadcast_to(ids[:, spot], (K, TILE))
            weights = soft_weights(dots, part, nrm, names, side * OWN_LISTS)
            there = (names < OWN_LISTS) if side == 0 else (names >= OWN_LISTS)
            out[:, spot] = jnp.where(there, weights, 0.0)
        return carry

    lax.fori_loop(0, COPIES, work, 0)


def assign_away_kernel(
    place, packed, members, ids, mine, near, far, wide, out, held, blocks, *scratch
):
    for shift, block in enumerate((mine, near, far, wide)):
        blocks[shift] = block[...]
    for seat in range(4):
        held[seat // 2, seat % 2 * HALF : (seat % 2 + 1) * HALF, :] = blocks[(place[1] - seat) & 3]
    assign_members(packed, members, ids, out, *scratch, 1)


def assign_own_kernel(packed, members, ids, out, *scratch):
    assign_members(packed, members, ids, out, *scratch, 0)


def assign_scratch(rows):
    return [
        pltpu.VMEM((OWN_LISTS * K, D), bf16),
        pltpu.VMEM((OWN_LISTS * K, LANES), f32),
        pltpu.VMEM((rows // TILE // COPIES, OWN_LISTS * K, TILE), f32),
        pltpu.VMEM((rows, D), bf16),
        pltpu.SemaphoreType.DMA((COPIES,)),
    ]


def assign_away(place, packed, members, ids, *blocks):
    rows = members.shape[0]
    return pl.pallas_call(
        assign_away_kernel,
        in_specs=[IN_SMEM, IN_VMEM, IN_PLACE, IN_VMEM] + [IN_VMEM] * 4,
        out_specs=[IN_VMEM, IN_VMEM],
        out_shape=[jax.ShapeDtypeStruct((K, rows), f32), jax.ShapeDtypeStruct((2, K, D), f32)],
        scratch_shapes=[pltpu.VMEM((4, HALF, D), f32)] + assign_scratch(rows),
        compiler_params=ROOM,
        name="assign_away",
    )(place, packed, members, ids, *blocks)


def assign_own(packed, members, ids):
    rows = members.shape[0]
    return pl.pallas_call(
        assign_own_kernel,
        in_specs=[IN_VMEM, IN_PLACE, IN_VMEM],
        out_specs=IN_VMEM,
        out_shape=jax.ShapeDtypeStruct((K, rows), f32),
        scratch_shapes=assign_scratch(rows),
        compiler_params=ROOM,
        name="assign_own",
    )(packed, members, ids)


SWAP = [(0, 1), (1, 0)]
SEAT_AXES = ("x", "z", "y")


def local(members, owner, seed_label):
    place = jnp.stack([lax.axis_index("c"), lax.axis_index("y")]).astype(jnp.int32)
    swap = lambda value: lax.ppermute(value, "c", SWAP)
    members, other, owner, seeds = (
        pltpu.with_memory_space_constraint(v, pltpu.HBM)
        for v in (members, swap(members), owner.reshape(1, -1), seed_label.reshape(1, -1))
    )

    def exchange(parts):
        return lax.all_to_all(parts, SEAT_AXES, split_axis=0, concat_axis=0, tiled=True)

    theirs, near_ids, code, held = seed_away(place, members, owner, seeds)
    parts, far_ids = lax.optimization_barrier((seed_own(code, held) + swap(theirs), swap(near_ids)))
    packed = exchange(finish(exchange(parts))[0])
    parts, held = first_round(packed, near_ids, other, far_ids, held)
    for turn in range(ITERS - 1):
        packed = exchange(finish(exchange(parts))[0])
        parts = later_round(packed, near_ids, held, far_ids)
    packed, exact = finish(exchange(parts))
    blocks = [exact] + [
        lax.ppermute(exact, "y", [(seat, (seat + shift) % 4) for seat in range(4)]) for shift in (1, 2, 3)
    ]
    packed = exchange(packed)
    given, centers = assign_away(place, packed, other, far_ids, *blocks)
    kept = assign_own(packed, members, near_ids)
    return kept + swap(given), centers


def solution(mesh):
    fine = Mesh(mesh.devices.reshape(4, 4, 2, 4), ("x", "z", "c", "y"))
    every = ("x", "z", "c", "y")
    return jax.shard_map(
        local,
        mesh=fine,
        in_specs=(P(every, None), P(every, None), P(every)),
        out_specs=(P(None, every), P(("x", "z", "c"), None, None)),
        check_vma=False,
    )
```

```python
import jax
import jax.numpy as jnp
from jax import lax
from jax.experimental import pallas as pl
from jax.experimental.pallas import tpu as pltpu
from jax.sharding import Mesh, PartitionSpec as P

K = 8
D = 768
ITERS = 3
HALF = K // 2
LANES = 128
CHUNK = D + LANES
OWN_LISTS = 32
SEATS = 64
TILE = 512
UNROLL = 8
COPIES = 4
SEED_COPIES = 4
f32 = jnp.float32
bf16 = jnp.bfloat16


def lane_fold(block):
    total = block[:, :LANES]
    for at in range(LANES, block.shape[1], LANES):
        total = total + block[:, at : at + LANES]
    return total


def store_sums(out, acc, tot, base):
    for seat in range(SEATS):
        row = base + seat * HALF
        out[seat, :, :D] = acc[row : row + HALF, :]
        out[seat, :, D:] = tot[row : row + HALF, :]


def relative(names, core):
    away = ((names >> 1) & 1) ^ core
    return (names >> 2) * 2 + (names & 1) + OWN_LISTS * away


def start_copies(sources, buf, sems, copies):
    rows = sources[0].shape[0] // copies
    for number in range(len(sources) * copies):
        source = sources[number // copies].at[pl.ds(number % copies * rows, rows), :]
        pltpu.make_async_copy(source, buf.at[pl.ds(number * rows, rows), :], sems.at[number]).start()


def wait_copy(source, buf, sems, copies, number):
    rows = source.shape[0] // copies
    pltpu.make_async_copy(
        source.at[pl.ds(0, rows), :], buf.at[pl.ds(number * rows, rows), :], sems.at[number]
    ).wait()


def at_tile(tile):
    return pl.ds(pl.multiple_of(tile * TILE, TILE), TILE)


def add_seeds(code, held, acc, tot, base, tile):
    spot = at_tile(tile)
    groups = lax.broadcasted_iota(jnp.int32, (K, TILE), 0)
    shifted = jnp.broadcast_to(code[:, spot], (K, TILE)) - groups
    rows = []
    for name in range(OWN_LISTS):
        hot = jnp.where(shifted == base + name * K, 1.0, 0.0).astype(f32)
        tot[name * K : (name + 1) * K, :] += lane_fold(hot)
        rows.append(hot)
    hots = jnp.concatenate(rows, axis=0).astype(bf16)
    acc[...] += jnp.dot(hots, held[spot, :], preferred_element_type=f32)


def seed_away_kernel(core, members, owner, seeds, theirs, ids, code, held, acc, tot, buf, sems, pair):
    start_copies([members], held, sems, SEED_COPIES)
    pltpu.make_async_copy(owner, ids, pair.at[0]).start()
    pltpu.make_async_copy(seeds, buf, pair.at[1]).start()
    acc[...] = jnp.zeros_like(acc)
    tot[...] = jnp.zeros_like(tot)
    pltpu.make_async_copy(owner, ids, pair.at[0]).wait()
    pltpu.make_async_copy(seeds, buf, pair.at[1]).wait()
    ids[...] = relative(ids[...], core[0])
    code[...] = ids[...] * K + buf[...]
    unroll = members.shape[0] // TILE // SEED_COPIES

    def work(turn, carry):
        wait_copy(members, held, sems, SEED_COPIES, turn)
        for part in range(unroll):
            add_seeds(code, held, acc, tot, OWN_LISTS * K, turn * unroll + part)
        return carry

    lax.fori_loop(0, SEED_COPIES, work, 0)
    store_sums(theirs, acc, tot, 0)


def seed_own_kernel(code, held, mine, acc, tot):
    acc[...] = jnp.zeros_like(acc)
    tot[...] = jnp.zeros_like(tot)
    for tile in range(code.shape[1] // TILE):
        add_seeds(code, held, acc, tot, 0, tile)
    store_sums(mine, acc, tot, 0)


IN_VMEM = pl.BlockSpec(memory_space=pltpu.VMEM)
IN_SMEM = pl.BlockSpec(memory_space=pltpu.SMEM)
IN_PLACE = pl.BlockSpec(memory_space=pltpu.HBM)


PART = jax.ShapeDtypeStruct((SEATS, HALF, CHUNK), f32)
SUM_SCRATCH = [pltpu.VMEM((OWN_LISTS * K, D), f32), pltpu.VMEM((OWN_LISTS * K, LANES), f32)]
ROOM = pltpu.CompilerParams(vmem_limit_bytes=36 << 20)


def seed_away(core, members, owner, seeds):
    rows = members.shape[0]
    names = jax.ShapeDtypeStruct((1, rows), jnp.int32)
    return pl.pallas_call(
        seed_away_kernel,
        in_specs=[IN_SMEM, IN_PLACE, IN_PLACE, IN_PLACE],
        out_specs=[IN_VMEM] * 4,
        out_shape=[PART, names, names, pltpu.VMEM((2 * rows, D), bf16)],
        scratch_shapes=SUM_SCRATCH
        + [
            pltpu.VMEM((1, rows), jnp.int32),
            pltpu.SemaphoreType.DMA((SEED_COPIES,)),
            pltpu.SemaphoreType.DMA((2,)),
        ],
        compiler_params=ROOM,
        name="seed_away",
    )(core, members, owner, seeds)


def seed_own(code, held):
    return pl.pallas_call(
        seed_own_kernel,
        in_specs=[IN_VMEM, IN_VMEM],
        out_specs=IN_VMEM,
        out_shape=PART,
        scratch_shapes=SUM_SCRATCH,
        compiler_params=ROOM,
        name="seed_own",
    )(code, held)


def finish_kernel(parts, out, exact):
    total = parts[0]
    for seat in range(1, SEATS):
        total = total + parts[seat]
    count = jnp.sum(total[:, D:], axis=1, keepdims=True)
    centers = total[:, :D] / (count + 1.0)
    exact[...] = centers
    norm = jnp.sum(centers * centers, axis=1, keepdims=True)
    lane = lax.broadcasted_iota(jnp.int32, (HALF, LANES), 1)
    norms = jnp.broadcast_to(norm, (HALF, LANES))
    high = norms.astype(bf16).astype(f32)
    middle = (norms - high).astype(bf16).astype(f32)
    low = norms - high - middle
    tail = jnp.where(lane == 0, high, jnp.where(lane == 1, middle, jnp.where(lane == 2, low, 0.0)))
    block = jnp.concatenate([centers, tail], axis=1).astype(bf16)
    for seat in range(SEATS):
        out[seat] = block


def finish(parts):
    return pl.pallas_call(
        finish_kernel,
        in_specs=[IN_VMEM],
        out_specs=[IN_VMEM, IN_VMEM],
        out_shape=[
            jax.ShapeDtypeStruct((SEATS, HALF, CHUNK), bf16),
            jax.ShapeDtypeStruct((HALF, D), f32),
        ],
        compiler_params=pltpu.CompilerParams(vmem_limit_bytes=4 << 20),
        name="finish",
    )(parts)


def unpack_centers(packed, cen, nrm):
    for group in range(OWN_LISTS // 2):
        blocks = [packed[4 * group + part].astype(f32) for part in range(4)]
        rows = slice(group * 2 * K, (group + 1) * 2 * K)
        cen[rows, :] = jnp.concatenate([b[:, :D] for b in blocks], axis=0).astype(bf16)
        tails = jnp.concatenate([b[:, D:] for b in blocks], axis=0)
        nrm[rows, :] = jnp.broadcast_to(jnp.sum(tails, axis=1, keepdims=True), (2 * K, LANES))


def dots_of(tile, cen, members):
    return lax.dot_general(
        cen[...], members[at_tile(tile), :], (((1,), (1,)), ((), ())), preferred_element_type=f32
    )


def soft_weights(dots, slot, nrm, names, offset):
    dot = jnp.zeros((K, TILE), f32)
    norm = jnp.zeros((K, TILE), f32)
    for name in range(OWN_LISTS):
        here = names == name + offset
        rows = slice(name * K, (name + 1) * K)
        dot = jnp.where(here, dots[slot, rows, :], dot)
        norm = jnp.where(here, jnp.concatenate([nrm[rows, :]] * (TILE // LANES), axis=1), norm)
    logits = (2.0 * dot - norm) / 2.0
    exps = jnp.exp(logits - jnp.max(logits, axis=0, keepdims=True))
    return exps / jnp.sum(exps, axis=0, keepdims=True)


def add_members(near_ids, far_ids, held, ids, cen, nrm, acc, tot, dots, arrive):
    half = near_ids.shape[1]
    ids[:, :half] = near_ids[...]
    ids[:, half:] = far_ids[...] ^ OWN_LISTS
    acc[...] = jnp.zeros_like(acc)
    tot[...] = jnp.zeros_like(tot)

    def work(turn, carry):
        arrive(turn)
        for part in range(UNROLL):
            dots[part] = dots_of(turn * UNROLL + part, cen, held)
        for part in range(UNROLL):
            spot = at_tile(turn * UNROLL + part)
            names = jnp.broadcast_to(ids[:, spot], (K, TILE))
            weights = soft_weights(dots, part, nrm, names, 0).astype(bf16).astype(f32)
            rows = []
            for name in range(OWN_LISTS):
                here = jnp.where(names == name, weights, 0.0)
                tot[name * K : (name + 1) * K, :] += lane_fold(here)
                rows.append(here)
            spread = jnp.concatenate(rows, axis=0).astype(bf16)
            acc[...] += jnp.dot(spread, held[spot, :], preferred_element_type=f32)
        return carry

    lax.fori_loop(0, held.shape[0] // TILE // UNROLL, work, 0)


def first_kernel(packed, near_ids, other, far_ids, before, out, held, cen, nrm, acc, tot, ids, dots, sems):
    rows = other.shape[0] // COPIES

    def copy_of(number):
        place = pl.ds(number * rows, rows)
        target = pl.ds(other.shape[0] + number * rows, rows)
        return pltpu.make_async_copy(other.at[place, :], held.at[target, :], sems.at[number])

    for number in range(COPIES):
        copy_of(number).start()
    unpack_centers(packed, cen, nrm)

    def arrive(turn):
        @pl.when(turn == other.shape[0] // TILE // UNROLL)
        def _():
            for number in range(COPIES):
                copy_of(number).wait()

    add_members(near_ids, far_ids, held, ids, cen, nrm, acc, tot, dots, arrive)
    store_sums(out, acc, tot, 0)


def later_kernel(packed, near_ids, held, far_ids, out, cen, nrm, acc, tot, ids, dots):
    unpack_centers(packed, cen, nrm)
    add_members(near_ids, far_ids, held, ids, cen, nrm, acc, tot, dots, lambda turn: None)
    store_sums(out, acc, tot, 0)


def round_scratch(rows):
    return [
        pltpu.VMEM((OWN_LISTS * K, D), bf16),
        pltpu.VMEM((OWN_LISTS * K, LANES), f32),
        pltpu.VMEM((OWN_LISTS * K, D), f32),
        pltpu.VMEM((OWN_LISTS * K, LANES), f32),
        pltpu.VMEM((1, 2 * rows), jnp.int32),
        pltpu.VMEM((UNROLL, OWN_LISTS * K, TILE), f32),
    ]


def first_round(packed, near_ids, other, far_ids, held):
    rows = other.shape[0]
    return pl.pallas_call(
        first_kernel,
        in_specs=[IN_VMEM, IN_VMEM, IN_PLACE, IN_VMEM, IN_VMEM],
        out_specs=[IN_VMEM, IN_VMEM],
        out_shape=[jax.ShapeDtypeStruct((SEATS, HALF, CHUNK), f32), pltpu.VMEM((2 * rows, D), bf16)],
        input_output_aliases={4: 1},
        scratch_shapes=round_scratch(rows) + [pltpu.SemaphoreType.DMA((COPIES,))],
        compiler_params=pltpu.CompilerParams(vmem_limit_bytes=36 << 20),
        name="first_round",
    )(packed, near_ids, other, far_ids, held)


def later_round(packed, near_ids, held, far_ids):
    return pl.pallas_call(
        later_kernel,
        in_specs=[IN_VMEM] * 4,
        out_specs=IN_VMEM,
        out_shape=jax.ShapeDtypeStruct((SEATS, HALF, CHUNK), f32),
        scratch_shapes=round_scratch(held.shape[0] // 2),
        compiler_params=pltpu.CompilerParams(vmem_limit_bytes=36 << 20),
        name="later_round",
    )(packed, near_ids, held, far_ids)


def assign_members(packed, members, ids, out, cen, nrm, dots, buf, sems, side):
    start_copies([members], buf, sems, COPIES)
    unpack_centers(packed, cen, nrm)
    group = members.shape[0] // TILE // COPIES

    def work(turn, carry):
        wait_copy(members, buf, sems, COPIES, turn)
        for part in range(group):
            dots[part] = dots_of(turn * group + part, cen, buf)
        for part in range(group):
            spot = at_tile(turn * group + part)
            names = jnp.broadcast_to(ids[:, spot], (K, TILE))
            weights = soft_weights(dots, part, nrm, names, side * OWN_LISTS)
            there = (names < OWN_LISTS) if side == 0 else (names >= OWN_LISTS)
            out[:, spot] = jnp.where(there, weights, 0.0)
        return carry

    lax.fori_loop(0, COPIES, work, 0)


def assign_away_kernel(
    place, packed, members, ids, mine, near, far, wide, out, held, blocks, *scratch
):
    for shift, block in enumerate((mine, near, far, wide)):
        blocks[shift] = block[...]
    for seat in range(4):
        held[seat // 2, seat % 2 * HALF : (seat % 2 + 1) * HALF, :] = blocks[(place[1] - seat) & 3]
    assign_members(packed, members, ids, out, *scratch, 1)


def assign_own_kernel(packed, members, ids, out, *scratch):
    assign_members(packed, members, ids, out, *scratch, 0)


def assign_scratch(rows):
    return [
        pltpu.VMEM((OWN_LISTS * K, D), bf16),
        pltpu.VMEM((OWN_LISTS * K, LANES), f32),
        pltpu.VMEM((rows // TILE // COPIES, OWN_LISTS * K, TILE), f32),
        pltpu.VMEM((rows, D), bf16),
        pltpu.SemaphoreType.DMA((COPIES,)),
    ]


def assign_away(place, packed, members, ids, *blocks):
    rows = members.shape[0]
    return pl.pallas_call(
        assign_away_kernel,
        in_specs=[IN_SMEM, IN_VMEM, IN_PLACE, IN_VMEM] + [IN_VMEM] * 4,
        out_specs=[IN_VMEM, IN_VMEM],
        out_shape=[jax.ShapeDtypeStruct((K, rows), f32), jax.ShapeDtypeStruct((2, K, D), f32)],
        scratch_shapes=[pltpu.VMEM((4, HALF, D), f32)] + assign_scratch(rows),
        compiler_params=ROOM,
        name="assign_away",
    )(place, packed, members, ids, *blocks)


def assign_own(packed, members, ids):
    rows = members.shape[0]
    return pl.pallas_call(
        assign_own_kernel,
        in_specs=[IN_VMEM, IN_PLACE, IN_VMEM],
        out_specs=IN_VMEM,
        out_shape=jax.ShapeDtypeStruct((K, rows), f32),
        scratch_shapes=assign_scratch(rows),
        compiler_params=ROOM,
        name="assign_own",
    )(packed, members, ids)


SWAP = [(0, 1), (1, 0)]
SEAT_AXES = ("x", "z", "y")


def local(members, owner, seed_label):
    place = jnp.stack([lax.axis_index("c"), lax.axis_index("y")]).astype(jnp.int32)
    swap = lambda value: lax.ppermute(value, "c", SWAP)
    place_in_hbm = lambda value: pltpu.with_memory_space_constraint(value, pltpu.HBM)
    members, owner, seeds = map(place_in_hbm, (members, owner.reshape(1, -1), seed_label.reshape(1, -1)))

    def exchange(parts):
        return lax.all_to_all(parts, SEAT_AXES, split_axis=0, concat_axis=0, tiled=True)

    theirs, near_ids, code, held = seed_away(place, members, owner, seeds)
    parts, far_ids, later = lax.optimization_barrier(
        (seed_own(code, held) + swap(theirs), swap(near_ids), members)
    )
    other = place_in_hbm(swap(later))
    packed = exchange(finish(exchange(parts))[0])
    parts, held = first_round(packed, near_ids, other, far_ids, held)
    for turn in range(ITERS - 1):
        packed = exchange(finish(exchange(parts))[0])
        parts = later_round(packed, near_ids, held, far_ids)
    packed, exact = finish(exchange(parts))
    blocks = [exact] + [
        lax.ppermute(exact, "y", [(seat, (seat + shift) % 4) for seat in range(4)]) for shift in (1, 2, 3)
    ]
    packed = exchange(packed)
    given, centers = assign_away(place, packed, other, far_ids, *blocks)
    kept = assign_own(packed, members, near_ids)
    return kept + swap(given), centers


def solution(mesh):
    fine = Mesh(mesh.devices.reshape(4, 4, 2, 4), ("x", "z", "c", "y"))
    every = ("x", "z", "c", "y")
    return jax.shard_map(
        local,
        mesh=fine,
        in_specs=(P(every, None), P(every, None), P(every)),
        out_specs=(P(None, every), P(("x", "z", "c"), None, None)),
        check_vma=False,
    )
```

```python
import jax
import jax.numpy as jnp
from jax import lax
from jax.experimental import pallas as pl
from jax.experimental.pallas import tpu as pltpu
from jax.sharding import Mesh, PartitionSpec as P

K = 8
D = 768
ITERS = 3
HALF = K // 2
LANES = 128
CHUNK = D + LANES
OWN_LISTS = 32
SEATS = 64
TILE = 512
UNROLL = 8
COPIES = 4
SEED_COPIES = 4
f32 = jnp.float32
bf16 = jnp.bfloat16


def lane_fold(block):
    total = block[:, :LANES]
    for at in range(LANES, block.shape[1], LANES):
        total = total + block[:, at : at + LANES]
    return total


def store_sums(out, acc, tot, base):
    for seat in range(SEATS):
        row = base + seat * HALF
        out[seat, :, :D] = acc[row : row + HALF, :]
        out[seat, :, D:] = tot[row : row + HALF, :]


def relative(names, core):
    away = ((names >> 1) & 1) ^ core
    return (names >> 2) * 2 + (names & 1) + OWN_LISTS * away


def start_copies(sources, buf, sems, copies):
    rows = sources[0].shape[0] // copies
    for number in range(len(sources) * copies):
        source = sources[number // copies].at[pl.ds(number % copies * rows, rows), :]
        pltpu.make_async_copy(source, buf.at[pl.ds(number * rows, rows), :], sems.at[number]).start()


def wait_copy(source, buf, sems, copies, number):
    rows = source.shape[0] // copies
    pltpu.make_async_copy(
        source.at[pl.ds(0, rows), :], buf.at[pl.ds(number * rows, rows), :], sems.at[number]
    ).wait()


def at_tile(tile):
    return pl.ds(pl.multiple_of(tile * TILE, TILE), TILE)


def add_seeds(code, held, acc, tot, base, tile):
    spot = at_tile(tile)
    groups = lax.broadcasted_iota(jnp.int32, (K, TILE), 0)
    shifted = jnp.broadcast_to(code[:, spot], (K, TILE)) - groups
    rows = []
    for name in range(OWN_LISTS):
        hot = jnp.where(shifted == base + name * K, 1.0, 0.0).astype(f32)
        tot[name * K : (name + 1) * K, :] += lane_fold(hot)
        rows.append(hot)
    hots = jnp.concatenate(rows, axis=0).astype(bf16)
    acc[...] += jnp.dot(hots, held[spot, :], preferred_element_type=f32)


def seed_away_kernel(core, members, owner, seeds, theirs, ids, code, held, acc, tot, buf, sems, pair):
    start_copies([members], held, sems, SEED_COPIES)
    pltpu.make_async_copy(owner, ids, pair.at[0]).start()
    pltpu.make_async_copy(seeds, buf, pair.at[1]).start()
    acc[...] = jnp.zeros_like(acc)
    tot[...] = jnp.zeros_like(tot)
    pltpu.make_async_copy(owner, ids, pair.at[0]).wait()
    pltpu.make_async_copy(seeds, buf, pair.at[1]).wait()
    ids[...] = relative(ids[...], core[0])
    code[...] = ids[...] * K + buf[...]
    unroll = members.shape[0] // TILE // SEED_COPIES

    def work(turn, carry):
        wait_copy(members, held, sems, SEED_COPIES, turn)
        for part in range(unroll):
            add_seeds(code, held, acc, tot, OWN_LISTS * K, turn * unroll + part)
        return carry

    lax.fori_loop(0, SEED_COPIES, work, 0)
    store_sums(theirs, acc, tot, 0)


def seed_own_kernel(code, held, mine, acc, tot):
    acc[...] = jnp.zeros_like(acc)
    tot[...] = jnp.zeros_like(tot)
    for tile in range(code.shape[1] // TILE):
        add_seeds(code, held, acc, tot, 0, tile)
    store_sums(mine, acc, tot, 0)


IN_VMEM = pl.BlockSpec(memory_space=pltpu.VMEM)
IN_SMEM = pl.BlockSpec(memory_space=pltpu.SMEM)
IN_PLACE = pl.BlockSpec(memory_space=pltpu.HBM)


PART = jax.ShapeDtypeStruct((SEATS, HALF, CHUNK), f32)
SUM_SCRATCH = [pltpu.VMEM((OWN_LISTS * K, D), f32), pltpu.VMEM((OWN_LISTS * K, LANES), f32)]
ROOM = pltpu.CompilerParams(vmem_limit_bytes=36 << 20)


def seed_away(core, members, owner, seeds):
    rows = members.shape[0]
    names = jax.ShapeDtypeStruct((1, rows), jnp.int32)
    return pl.pallas_call(
        seed_away_kernel,
        in_specs=[IN_SMEM, IN_PLACE, IN_PLACE, IN_PLACE],
        out_specs=[IN_VMEM] * 4,
        out_shape=[PART, names, names, pltpu.VMEM((2 * rows, D), bf16)],
        scratch_shapes=SUM_SCRATCH
        + [
            pltpu.VMEM((1, rows), jnp.int32),
            pltpu.SemaphoreType.DMA((SEED_COPIES,)),
            pltpu.SemaphoreType.DMA((2,)),
        ],
        compiler_params=ROOM,
        name="seed_away",
    )(core, members, owner, seeds)


def seed_own(code, held):
    return pl.pallas_call(
        seed_own_kernel,
        in_specs=[IN_VMEM, IN_VMEM],
        out_specs=IN_VMEM,
        out_shape=PART,
        scratch_shapes=SUM_SCRATCH,
        compiler_params=ROOM,
        name="seed_own",
    )(code, held)


def finish_kernel(parts, out, exact):
    total = parts[0]
    for seat in range(1, SEATS):
        total = total + parts[seat]
    count = jnp.sum(total[:, D:], axis=1, keepdims=True)
    centers = total[:, :D] / (count + 1.0)
    exact[...] = centers
    norm = jnp.sum(centers * centers, axis=1, keepdims=True)
    lane = lax.broadcasted_iota(jnp.int32, (HALF, LANES), 1)
    norms = jnp.broadcast_to(norm, (HALF, LANES))
    high = norms.astype(bf16).astype(f32)
    middle = (norms - high).astype(bf16).astype(f32)
    low = norms - high - middle
    tail = jnp.where(lane == 0, high, jnp.where(lane == 1, middle, jnp.where(lane == 2, low, 0.0)))
    block = jnp.concatenate([centers, tail], axis=1).astype(bf16)
    for seat in range(SEATS):
        out[seat] = block


def finish(parts):
    return pl.pallas_call(
        finish_kernel,
        in_specs=[IN_VMEM],
        out_specs=[IN_VMEM, IN_VMEM],
        out_shape=[
            jax.ShapeDtypeStruct((SEATS, HALF, CHUNK), bf16),
            jax.ShapeDtypeStruct((HALF, D), f32),
        ],
        compiler_params=pltpu.CompilerParams(vmem_limit_bytes=4 << 20),
        name="finish",
    )(parts)


def unpack_centers(packed, cen, nrm):
    for group in range(OWN_LISTS // 2):
        blocks = [packed[4 * group + part].astype(f32) for part in range(4)]
        rows = slice(group * 2 * K, (group + 1) * 2 * K)
        cen[rows, :] = jnp.concatenate([b[:, :D] for b in blocks], axis=0).astype(bf16)
        tails = jnp.concatenate([b[:, D:] for b in blocks], axis=0)
        nrm[rows, :] = jnp.broadcast_to(jnp.sum(tails, axis=1, keepdims=True), (2 * K, LANES))


def dots_of(tile, cen, members):
    return lax.dot_general(
        cen[...], members[at_tile(tile), :], (((1,), (1,)), ((), ())), preferred_element_type=f32
    )


def soft_weights(dots, slot, nrm, names, offset):
    dot = jnp.zeros((K, TILE), f32)
    norm = jnp.zeros((K, TILE), f32)
    for name in range(OWN_LISTS):
        here = names == name + offset
        rows = slice(name * K, (name + 1) * K)
        dot = jnp.where(here, dots[slot, rows, :], dot)
        norm = jnp.where(here, jnp.concatenate([nrm[rows, :]] * (TILE // LANES), axis=1), norm)
    logits = (2.0 * dot - norm) / 2.0
    exps = jnp.exp(logits - jnp.max(logits, axis=0, keepdims=True))
    return exps / jnp.sum(exps, axis=0, keepdims=True)


def add_members(near_ids, far_ids, held, ids, cen, nrm, acc, tot, dots, flat, arrive):
    half = near_ids.shape[1]
    ids[:, :half] = near_ids[...]
    ids[:, half:] = far_ids[...] ^ OWN_LISTS
    flat[...] = cen[...].T
    acc[...] = jnp.zeros_like(acc)
    tot[...] = jnp.zeros_like(tot)

    def work(turn, carry):
        arrive(turn)
        for part in range(UNROLL):
            tile = held[at_tile(turn * UNROLL + part), :]
            dots[part] = jnp.dot(tile, flat[...], preferred_element_type=f32).T
        for part in range(UNROLL):
            spot = at_tile(turn * UNROLL + part)
            names = jnp.broadcast_to(ids[:, spot], (K, TILE))
            weights = soft_weights(dots, part, nrm, names, 0).astype(bf16).astype(f32)
            rows = []
            for name in range(OWN_LISTS):
                here = jnp.where(names == name, weights, 0.0)
                tot[name * K : (name + 1) * K, :] += lane_fold(here)
                rows.append(here)
            spread = jnp.concatenate(rows, axis=0).astype(bf16)
            acc[...] += jnp.dot(spread, held[spot, :], preferred_element_type=f32)
        return carry

    lax.fori_loop(0, held.shape[0] // TILE // UNROLL, work, 0)


def first_kernel(packed, near_ids, other, far_ids, before, out, held, cen, nrm, acc, tot, ids, dots, flat, sems):
    rows = other.shape[0] // COPIES

    def copy_of(number):
        place = pl.ds(number * rows, rows)
        target = pl.ds(other.shape[0] + number * rows, rows)
        return pltpu.make_async_copy(other.at[place, :], held.at[target, :], sems.at[number])

    for number in range(COPIES):
        copy_of(number).start()
    unpack_centers(packed, cen, nrm)

    def arrive(turn):
        @pl.when(turn == other.shape[0] // TILE // UNROLL)
        def _():
            for number in range(COPIES):
                copy_of(number).wait()

    add_members(near_ids, far_ids, held, ids, cen, nrm, acc, tot, dots, flat, arrive)
    store_sums(out, acc, tot, 0)


def later_kernel(packed, near_ids, held, far_ids, out, cen, nrm, acc, tot, ids, dots, flat):
    unpack_centers(packed, cen, nrm)
    add_members(near_ids, far_ids, held, ids, cen, nrm, acc, tot, dots, flat, lambda turn: None)
    store_sums(out, acc, tot, 0)


def round_scratch(rows):
    return [
        pltpu.VMEM((OWN_LISTS * K, D), bf16),
        pltpu.VMEM((OWN_LISTS * K, LANES), f32),
        pltpu.VMEM((OWN_LISTS * K, D), f32),
        pltpu.VMEM((OWN_LISTS * K, LANES), f32),
        pltpu.VMEM((1, 2 * rows), jnp.int32),
        pltpu.VMEM((UNROLL, OWN_LISTS * K, TILE), f32),
        pltpu.VMEM((D, OWN_LISTS * K), bf16),
    ]


def first_round(packed, near_ids, other, far_ids, held):
    rows = other.shape[0]
    return pl.pallas_call(
        first_kernel,
        in_specs=[IN_VMEM, IN_VMEM, IN_PLACE, IN_VMEM, IN_VMEM],
        out_specs=[IN_VMEM, IN_VMEM],
        out_shape=[jax.ShapeDtypeStruct((SEATS, HALF, CHUNK), f32), pltpu.VMEM((2 * rows, D), bf16)],
        input_output_aliases={4: 1},
        scratch_shapes=round_scratch(rows) + [pltpu.SemaphoreType.DMA((COPIES,))],
        compiler_params=pltpu.CompilerParams(vmem_limit_bytes=36 << 20),
        name="first_round",
    )(packed, near_ids, other, far_ids, held)


def later_round(packed, near_ids, held, far_ids):
    return pl.pallas_call(
        later_kernel,
        in_specs=[IN_VMEM] * 4,
        out_specs=IN_VMEM,
        out_shape=jax.ShapeDtypeStruct((SEATS, HALF, CHUNK), f32),
        scratch_shapes=round_scratch(held.shape[0] // 2),
        compiler_params=pltpu.CompilerParams(vmem_limit_bytes=36 << 20),
        name="later_round",
    )(packed, near_ids, held, far_ids)


def assign_members(packed, members, ids, out, cen, nrm, dots, buf, sems, side):
    start_copies([members], buf, sems, COPIES)
    unpack_centers(packed, cen, nrm)
    group = members.shape[0] // TILE // COPIES

    def work(turn, carry):
        wait_copy(members, buf, sems, COPIES, turn)
        for part in range(group):
            dots[part] = dots_of(turn * group + part, cen, buf)
        for part in range(group):
            spot = at_tile(turn * group + part)
            names = jnp.broadcast_to(ids[:, spot], (K, TILE))
            weights = soft_weights(dots, part, nrm, names, side * OWN_LISTS)
            there = (names < OWN_LISTS) if side == 0 else (names >= OWN_LISTS)
            out[:, spot] = jnp.where(there, weights, 0.0)
        return carry

    lax.fori_loop(0, COPIES, work, 0)


def assign_away_kernel(
    place, packed, members, ids, mine, near, far, wide, out, held, blocks, *scratch
):
    for shift, block in enumerate((mine, near, far, wide)):
        blocks[shift] = block[...]
    for seat in range(4):
        held[seat // 2, seat % 2 * HALF : (seat % 2 + 1) * HALF, :] = blocks[(place[1] - seat) & 3]
    assign_members(packed, members, ids, out, *scratch, 1)


def assign_own_kernel(packed, members, ids, out, *scratch):
    assign_members(packed, members, ids, out, *scratch, 0)


def assign_scratch(rows):
    return [
        pltpu.VMEM((OWN_LISTS * K, D), bf16),
        pltpu.VMEM((OWN_LISTS * K, LANES), f32),
        pltpu.VMEM((rows // TILE // COPIES, OWN_LISTS * K, TILE), f32),
        pltpu.VMEM((rows, D), bf16),
        pltpu.SemaphoreType.DMA((COPIES,)),
    ]


def assign_away(place, packed, members, ids, *blocks):
    rows = members.shape[0]
    return pl.pallas_call(
        assign_away_kernel,
        in_specs=[IN_SMEM, IN_VMEM, IN_PLACE, IN_VMEM] + [IN_VMEM] * 4,
        out_specs=[IN_VMEM, IN_VMEM],
        out_shape=[jax.ShapeDtypeStruct((K, rows), f32), jax.ShapeDtypeStruct((2, K, D), f32)],
        scratch_shapes=[pltpu.VMEM((4, HALF, D), f32)] + assign_scratch(rows),
        compiler_params=ROOM,
        name="assign_away",
    )(place, packed, members, ids, *blocks)


def assign_own(packed, members, ids):
    rows = members.shape[0]
    return pl.pallas_call(
        assign_own_kernel,
        in_specs=[IN_VMEM, IN_PLACE, IN_VMEM],
        out_specs=IN_VMEM,
        out_shape=jax.ShapeDtypeStruct((K, rows), f32),
        scratch_shapes=assign_scratch(rows),
        compiler_params=ROOM,
        name="assign_own",
    )(packed, members, ids)


SWAP = [(0, 1), (1, 0)]
SEAT_AXES = ("x", "z", "y")


def local(members, owner, seed_label):
    place = jnp.stack([lax.axis_index("c"), lax.axis_index("y")]).astype(jnp.int32)
    swap = lambda value: lax.ppermute(value, "c", SWAP)
    place_in_hbm = lambda value: pltpu.with_memory_space_constraint(value, pltpu.HBM)
    members, owner, seeds = map(place_in_hbm, (members, owner.reshape(1, -1), seed_label.reshape(1, -1)))

    def exchange(parts):
        return lax.all_to_all(parts, SEAT_AXES, split_axis=0, concat_axis=0, tiled=True)

    theirs, near_ids, code, held = seed_away(place, members, owner, seeds)
    parts, far_ids, later = lax.optimization_barrier(
        (seed_own(code, held) + swap(theirs), swap(near_ids), members)
    )
    other = place_in_hbm(swap(later))
    packed = exchange(finish(exchange(parts))[0])
    parts, held = first_round(packed, near_ids, other, far_ids, held)
    for turn in range(ITERS - 1):
        packed = exchange(finish(exchange(parts))[0])
        parts = later_round(packed, near_ids, held, far_ids)
    packed, exact = finish(exchange(parts))
    blocks = [exact] + [
        lax.ppermute(exact, "y", [(seat, (seat + shift) % 4) for seat in range(4)]) for shift in (1, 2, 3)
    ]
    packed = exchange(packed)
    given, centers = assign_away(place, packed, other, far_ids, *blocks)
    kept = assign_own(packed, members, near_ids)
    return kept + swap(given), centers


def solution(mesh):
    fine = Mesh(mesh.devices.reshape(4, 4, 2, 4), ("x", "z", "c", "y"))
    every = ("x", "z", "c", "y")
    return jax.shard_map(
        local,
        mesh=fine,
        in_specs=(P(every, None), P(every, None), P(every)),
        out_specs=(P(None, every), P(("x", "z", "c"), None, None)),
        check_vma=False,
    )
```

```python
import jax
import jax.numpy as jnp
from jax import lax
from jax.experimental import pallas as pl
from jax.experimental.pallas import tpu as pltpu
from jax.sharding import Mesh, PartitionSpec as P

K = 8
D = 768
ITERS = 3
HALF = K // 2
LANES = 128
CHUNK = D + LANES
OWN_LISTS = 32
SEATS = 64
TILE = 512
UNROLL = 8
COPIES = 2
SEED_COPIES = 4
f32 = jnp.float32
bf16 = jnp.bfloat16


def lane_fold(block):
    total = block[:, :LANES]
    for at in range(LANES, block.shape[1], LANES):
        total = total + block[:, at : at + LANES]
    return total


def store_sums(out, acc, tot, base):
    for seat in range(SEATS):
        row = base + seat * HALF
        out[seat, :, :D] = acc[row : row + HALF, :]
        out[seat, :, D:] = tot[row : row + HALF, :]


def relative(names, core):
    away = ((names >> 1) & 1) ^ core
    return (names >> 2) * 2 + (names & 1) + OWN_LISTS * away


def start_copies(sources, buf, sems, copies):
    rows = sources[0].shape[0] // copies
    for number in range(len(sources) * copies):
        source = sources[number // copies].at[pl.ds(number % copies * rows, rows), :]
        pltpu.make_async_copy(source, buf.at[pl.ds(number * rows, rows), :], sems.at[number]).start()


def wait_copy(source, buf, sems, copies, number):
    rows = source.shape[0] // copies
    pltpu.make_async_copy(
        source.at[pl.ds(0, rows), :], buf.at[pl.ds(number * rows, rows), :], sems.at[number]
    ).wait()


def at_tile(tile):
    return pl.ds(pl.multiple_of(tile * TILE, TILE), TILE)


def add_seeds(code, held, acc, tot, base, tile):
    spot = at_tile(tile)
    groups = lax.broadcasted_iota(jnp.int32, (K, TILE), 0)
    shifted = jnp.broadcast_to(code[:, spot], (K, TILE)) - groups
    rows = []
    for name in range(OWN_LISTS):
        hot = jnp.where(shifted == base + name * K, 1.0, 0.0).astype(f32)
        tot[name * K : (name + 1) * K, :] += lane_fold(hot)
        rows.append(hot)
    hots = jnp.concatenate(rows, axis=0).astype(bf16)
    acc[...] += jnp.dot(hots, held[spot, :], preferred_element_type=f32)


def seed_away_kernel(core, members, owner, seeds, theirs, ids, code, held, acc, tot, buf, sems, pair):
    start_copies([members], held, sems, SEED_COPIES)
    pltpu.make_async_copy(owner, ids, pair.at[0]).start()
    pltpu.make_async_copy(seeds, buf, pair.at[1]).start()
    acc[...] = jnp.zeros_like(acc)
    tot[...] = jnp.zeros_like(tot)
    pltpu.make_async_copy(owner, ids, pair.at[0]).wait()
    pltpu.make_async_copy(seeds, buf, pair.at[1]).wait()
    ids[...] = relative(ids[...], core[0])
    code[...] = ids[...] * K + buf[...]
    unroll = members.shape[0] // TILE // SEED_COPIES

    def work(turn, carry):
        wait_copy(members, held, sems, SEED_COPIES, turn)
        for part in range(unroll):
            add_seeds(code, held, acc, tot, OWN_LISTS * K, turn * unroll + part)
        return carry

    lax.fori_loop(0, SEED_COPIES, work, 0)
    store_sums(theirs, acc, tot, 0)


def seed_own_kernel(code, held, mine, acc, tot):
    acc[...] = jnp.zeros_like(acc)
    tot[...] = jnp.zeros_like(tot)
    for tile in range(code.shape[1] // TILE):
        add_seeds(code, held, acc, tot, 0, tile)
    store_sums(mine, acc, tot, 0)


IN_VMEM = pl.BlockSpec(memory_space=pltpu.VMEM)
IN_SMEM = pl.BlockSpec(memory_space=pltpu.SMEM)
IN_PLACE = pl.BlockSpec(memory_space=pltpu.HBM)


PART = jax.ShapeDtypeStruct((SEATS, HALF, CHUNK), f32)
SUM_SCRATCH = [pltpu.VMEM((OWN_LISTS * K, D), f32), pltpu.VMEM((OWN_LISTS * K, LANES), f32)]
ROOM = pltpu.CompilerParams(vmem_limit_bytes=36 << 20)


def seed_away(core, members, owner, seeds):
    rows = members.shape[0]
    names = jax.ShapeDtypeStruct((1, rows), jnp.int32)
    return pl.pallas_call(
        seed_away_kernel,
        in_specs=[IN_SMEM, IN_PLACE, IN_PLACE, IN_PLACE],
        out_specs=[IN_VMEM] * 4,
        out_shape=[PART, names, names, pltpu.VMEM((2 * rows, D), bf16)],
        scratch_shapes=SUM_SCRATCH
        + [
            pltpu.VMEM((1, rows), jnp.int32),
            pltpu.SemaphoreType.DMA((SEED_COPIES,)),
            pltpu.SemaphoreType.DMA((2,)),
        ],
        compiler_params=ROOM,
        name="seed_away",
    )(core, members, owner, seeds)


def seed_own(code, held):
    return pl.pallas_call(
        seed_own_kernel,
        in_specs=[IN_VMEM, IN_VMEM],
        out_specs=IN_VMEM,
        out_shape=PART,
        scratch_shapes=SUM_SCRATCH,
        compiler_params=ROOM,
        name="seed_own",
    )(code, held)


def finish_kernel(parts, out, exact):
    total = parts[0]
    for seat in range(1, SEATS):
        total = total + parts[seat]
    count = jnp.sum(total[:, D:], axis=1, keepdims=True)
    centers = total[:, :D] / (count + 1.0)
    exact[...] = centers
    norm = jnp.sum(centers * centers, axis=1, keepdims=True)
    lane = lax.broadcasted_iota(jnp.int32, (HALF, LANES), 1)
    norms = jnp.broadcast_to(norm, (HALF, LANES))
    high = norms.astype(bf16).astype(f32)
    middle = (norms - high).astype(bf16).astype(f32)
    low = norms - high - middle
    tail = jnp.where(lane == 0, high, jnp.where(lane == 1, middle, jnp.where(lane == 2, low, 0.0)))
    block = jnp.concatenate([centers, tail], axis=1).astype(bf16)
    for seat in range(SEATS):
        out[seat] = block


def finish(parts):
    return pl.pallas_call(
        finish_kernel,
        in_specs=[IN_VMEM],
        out_specs=[IN_VMEM, IN_VMEM],
        out_shape=[
            jax.ShapeDtypeStruct((SEATS, HALF, CHUNK), bf16),
            jax.ShapeDtypeStruct((HALF, D), f32),
        ],
        compiler_params=pltpu.CompilerParams(vmem_limit_bytes=4 << 20),
        name="finish",
    )(parts)


def unpack_centers(packed, cen, nrm):
    for group in range(OWN_LISTS // 2):
        blocks = [packed[4 * group + part].astype(f32) for part in range(4)]
        rows = slice(group * 2 * K, (group + 1) * 2 * K)
        cen[rows, :] = jnp.concatenate([b[:, :D] for b in blocks], axis=0).astype(bf16)
        tails = jnp.concatenate([b[:, D:] for b in blocks], axis=0)
        nrm[rows, :] = jnp.broadcast_to(jnp.sum(tails, axis=1, keepdims=True), (2 * K, LANES))


def dots_of(tile, cen, members):
    return lax.dot_general(
        cen[...], members[at_tile(tile), :], (((1,), (1,)), ((), ())), preferred_element_type=f32
    )


def soft_weights(dots, slot, nrm, names, offset):
    dot = jnp.zeros((K, TILE), f32)
    norm = jnp.zeros((K, TILE), f32)
    for name in range(OWN_LISTS):
        here = names == name + offset
        rows = slice(name * K, (name + 1) * K)
        dot = jnp.where(here, dots[slot, rows, :], dot)
        norm = jnp.where(here, jnp.concatenate([nrm[rows, :]] * (TILE // LANES), axis=1), norm)
    logits = (2.0 * dot - norm) / 2.0
    exps = jnp.exp(logits - jnp.max(logits, axis=0, keepdims=True))
    return exps / jnp.sum(exps, axis=0, keepdims=True)


def add_members(near_ids, far_ids, held, ids, cen, nrm, acc, tot, dots, arrive):
    half = near_ids.shape[1]
    ids[:, :half] = near_ids[...]
    ids[:, half:] = far_ids[...] ^ OWN_LISTS
    acc[...] = jnp.zeros_like(acc)
    tot[...] = jnp.zeros_like(tot)

    def work(turn, carry):
        arrive(turn)
        for part in range(UNROLL):
            dots[part] = dots_of(turn * UNROLL + part, cen, held)
        for part in range(UNROLL):
            spot = at_tile(turn * UNROLL + part)
            names = jnp.broadcast_to(ids[:, spot], (K, TILE))
            weights = soft_weights(dots, part, nrm, names, 0).astype(bf16).astype(f32)
            rows = []
            for name in range(OWN_LISTS):
                here = jnp.where(names == name, weights, 0.0)
                tot[name * K : (name + 1) * K, :] += lane_fold(here)
                rows.append(here)
            spread = jnp.concatenate(rows, axis=0).astype(bf16)
            acc[...] += jnp.dot(spread, held[spot, :], preferred_element_type=f32)
        return carry

    lax.fori_loop(0, held.shape[0] // TILE // UNROLL, work, 0)


def first_kernel(packed, near_ids, other, far_ids, before, out, held, cen, nrm, acc, tot, ids, dots, sems):
    rows = other.shape[0] // COPIES

    def copy_of(number):
        place = pl.ds(number * rows, rows)
        target = pl.ds(other.shape[0] + number * rows, rows)
        return pltpu.make_async_copy(other.at[place, :], held.at[target, :], sems.at[number])

    for number in range(COPIES):
        copy_of(number).start()
    unpack_centers(packed, cen, nrm)

    def arrive(turn):
        @pl.when(turn == other.shape[0] // TILE // UNROLL)
        def _():
            for number in range(COPIES):
                copy_of(number).wait()

    add_members(near_ids, far_ids, held, ids, cen, nrm, acc, tot, dots, arrive)
    store_sums(out, acc, tot, 0)


def later_kernel(packed, near_ids, held, far_ids, out, cen, nrm, acc, tot, ids, dots):
    unpack_centers(packed, cen, nrm)
    add_members(near_ids, far_ids, held, ids, cen, nrm, acc, tot, dots, lambda turn: None)
    store_sums(out, acc, tot, 0)


def round_scratch(rows):
    return [
        pltpu.VMEM((OWN_LISTS * K, D), bf16),
        pltpu.VMEM((OWN_LISTS * K, LANES), f32),
        pltpu.VMEM((OWN_LISTS * K, D), f32),
        pltpu.VMEM((OWN_LISTS * K, LANES), f32),
        pltpu.VMEM((1, 2 * rows), jnp.int32),
        pltpu.VMEM((UNROLL, OWN_LISTS * K, TILE), f32),
    ]


def first_round(packed, near_ids, other, far_ids, held):
    rows = other.shape[0]
    return pl.pallas_call(
        first_kernel,
        in_specs=[IN_VMEM, IN_VMEM, IN_PLACE, IN_VMEM, IN_VMEM],
        out_specs=[IN_VMEM, IN_VMEM],
        out_shape=[jax.ShapeDtypeStruct((SEATS, HALF, CHUNK), f32), pltpu.VMEM((2 * rows, D), bf16)],
        input_output_aliases={4: 1},
        scratch_shapes=round_scratch(rows) + [pltpu.SemaphoreType.DMA((COPIES,))],
        compiler_params=pltpu.CompilerParams(vmem_limit_bytes=36 << 20),
        name="first_round",
    )(packed, near_ids, other, far_ids, held)


def later_round(packed, near_ids, held, far_ids):
    return pl.pallas_call(
        later_kernel,
        in_specs=[IN_VMEM] * 4,
        out_specs=IN_VMEM,
        out_shape=jax.ShapeDtypeStruct((SEATS, HALF, CHUNK), f32),
        scratch_shapes=round_scratch(held.shape[0] // 2),
        compiler_params=pltpu.CompilerParams(vmem_limit_bytes=36 << 20),
        name="later_round",
    )(packed, near_ids, held, far_ids)


def assign_members(packed, members, ids, out, cen, nrm, dots, buf, sems, side):
    start_copies([members], buf, sems, COPIES)
    unpack_centers(packed, cen, nrm)
    group = members.shape[0] // TILE // COPIES

    def work(turn, carry):
        wait_copy(members, buf, sems, COPIES, turn)
        for part in range(group):
            dots[part] = dots_of(turn * group + part, cen, buf)
        for part in range(group):
            spot = at_tile(turn * group + part)
            names = jnp.broadcast_to(ids[:, spot], (K, TILE))
            weights = soft_weights(dots, part, nrm, names, side * OWN_LISTS)
            there = (names < OWN_LISTS) if side == 0 else (names >= OWN_LISTS)
            out[:, spot] = jnp.where(there, weights, 0.0)
        return carry

    lax.fori_loop(0, COPIES, work, 0)


def assign_away_kernel(
    place, packed, members, ids, mine, near, far, wide, out, held, blocks, *scratch
):
    for shift, block in enumerate((mine, near, far, wide)):
        blocks[shift] = block[...]
    for seat in range(4):
        held[seat // 2, seat % 2 * HALF : (seat % 2 + 1) * HALF, :] = blocks[(place[1] - seat) & 3]
    assign_members(packed, members, ids, out, *scratch, 1)


def assign_own_kernel(packed, members, ids, out, *scratch):
    assign_members(packed, members, ids, out, *scratch, 0)


def assign_scratch(rows):
    return [
        pltpu.VMEM((OWN_LISTS * K, D), bf16),
        pltpu.VMEM((OWN_LISTS * K, LANES), f32),
        pltpu.VMEM((rows // TILE // COPIES, OWN_LISTS * K, TILE), f32),
        pltpu.VMEM((rows, D), bf16),
        pltpu.SemaphoreType.DMA((COPIES,)),
    ]


def assign_away(place, packed, members, ids, *blocks):
    rows = members.shape[0]
    return pl.pallas_call(
        assign_away_kernel,
        in_specs=[IN_SMEM, IN_VMEM, IN_PLACE, IN_VMEM] + [IN_VMEM] * 4,
        out_specs=[IN_VMEM, IN_VMEM],
        out_shape=[jax.ShapeDtypeStruct((K, rows), f32), jax.ShapeDtypeStruct((2, K, D), f32)],
        scratch_shapes=[pltpu.VMEM((4, HALF, D), f32)] + assign_scratch(rows),
        compiler_params=ROOM,
        name="assign_away",
    )(place, packed, members, ids, *blocks)


def assign_own(packed, members, ids):
    rows = members.shape[0]
    return pl.pallas_call(
        assign_own_kernel,
        in_specs=[IN_VMEM, IN_PLACE, IN_VMEM],
        out_specs=IN_VMEM,
        out_shape=jax.ShapeDtypeStruct((K, rows), f32),
        scratch_shapes=assign_scratch(rows),
        compiler_params=ROOM,
        name="assign_own",
    )(packed, members, ids)


SWAP = [(0, 1), (1, 0)]
SEAT_AXES = ("x", "z", "y")


def local(members, owner, seed_label):
    place = jnp.stack([lax.axis_index("c"), lax.axis_index("y")]).astype(jnp.int32)
    swap = lambda value: lax.ppermute(value, "c", SWAP)
    place_in_hbm = lambda value: pltpu.with_memory_space_constraint(value, pltpu.HBM)
    members, owner, seeds = map(place_in_hbm, (members, owner.reshape(1, -1), seed_label.reshape(1, -1)))

    def exchange(parts):
        return lax.all_to_all(parts, SEAT_AXES, split_axis=0, concat_axis=0, tiled=True)

    theirs, near_ids, code, held = seed_away(place, members, owner, seeds)
    parts, far_ids, later = lax.optimization_barrier(
        (seed_own(code, held) + swap(theirs), swap(near_ids), members)
    )
    other = place_in_hbm(swap(later))
    packed = exchange(finish(exchange(parts))[0])
    parts, held = first_round(packed, near_ids, other, far_ids, held)
    for turn in range(ITERS - 1):
        packed = exchange(finish(exchange(parts))[0])
        parts = later_round(packed, near_ids, held, far_ids)
    packed, exact = finish(exchange(parts))
    blocks = [exact] + [
        lax.ppermute(exact, "y", [(seat, (seat + shift) % 4) for seat in range(4)]) for shift in (1, 2, 3)
    ]
    packed = exchange(packed)
    given, centers = assign_away(place, packed, other, far_ids, *blocks)
    kept = assign_own(packed, members, near_ids)
    return kept + swap(given), centers


def solution(mesh):
    fine = Mesh(mesh.devices.reshape(4, 4, 2, 4), ("x", "z", "c", "y"))
    every = ("x", "z", "c", "y")
    return jax.shard_map(
        local,
        mesh=fine,
        in_specs=(P(every, None), P(every, None), P(every)),
        out_specs=(P(None, every), P(("x", "z", "c"), None, None)),
        check_vma=False,
    )
```
